32 devices in a mesh: groups: 2 (over y), patch: 4 (over z), chan: 2 (over x), sub: 2 (over core).
Axes of the slice: x: 2, y: 2, z: 4, core: 2. Of those that a mesh axis runs over, the one named last changes fastest.
Arguments:
- latent: bfloat16 [640, 2048], P(('chan', 'sub'), ('groups', 'patch')), parts along dimension 1, may hold values from -18 to 18
- timestep: int32 [2], P('groups'), parts along dimension 0, may hold values from 0 to 999
- time_w1: bfloat16 [1280, 320], replicated, may hold values from -0.3125 to 0.3125
- time_proj: bfloat16 [640, 1280], P(('chan', 'sub')), may hold values from -0.15625 to 0.15625
- conv1_w: bfloat16 [9, 640, 640], P(None, ('chan', 'sub')), may hold values from -0.078125 to 0.078125
- conv2_w: bfloat16 [9, 640, 640], P(None, ('chan', 'sub')), may hold values from -0.078125 to 0.078125
- proj_in_w: bfloat16 [640, 640], P(('chan', 'sub')), may hold values from -0.25 to 0.25
- q_w: bfloat16 [640, 640], P(('chan', 'sub')), may hold values from -8 to 8
- kv_w: bfloat16 [2, 640, 640], P(None, ('chan', 'sub')), may hold values from -8 to 8
- out_w: bfloat16 [640, 640], P(('chan', 'sub')), may hold values from -0.25 to 0.25
- proj_out_w: bfloat16 [640, 640], P(('chan', 'sub')), may hold values from -0.25 to 0.25
Outputs:
- output: bfloat16 [640, 2048], P(('chan', 'sub'), ('groups', 'patch')), parts along dimension 1
The draws below stay inside these ranges and needn't reach their ends.
There are 2 independent parts, one for each index of `groups`. The reference program is written for one: setup_inputs(seed, part) draws one part's arguments, and reference() takes and returns one part's arrays. A program takes and returns all parts, laid end to end along the dimension named above; an argument that names none is the same for every part. Nothing has to cross between parts.
All inputs are finite; a program needn't handle non-finite values.
Results may differ from the reference program's by a relative error of at most 0.02.
Values may be sent and summed in bfloat16 or wider, within the bound.
No kernel may reach another device: no remote copies, remote signals or barrier semaphores. Data moves between devices by JAX's collectives and lax.ppermute only.
A program may use at most 64 MiB of HBM per device.

```python
import math
import jax
import jax.numpy as jnp
from jax import lax

C = 640
HEADS = 10
HEAD_DIM = 64
NGROUPS = 32
TEMB = 1280
FREQ = 320
WIDTH = 256
TOKENS = 1024


def draw_latent(key, part):
    height = TOKENS // WIDTH
    subkeys = jax.random.split(key, 4)
    row_index = (jnp.arange(TOKENS) // WIDTH).astype(jnp.float32)
    row_slope = row_index / max(height - 1, 1)
    base_noise = jnp.clip(jax.random.normal(subkeys[0], (C, TOKENS), jnp.float32), -4.0, 4.0)
    log_level = 0.5 * row_slope + 0.5 * jax.random.uniform(subkeys[1], (TOKENS,), jnp.float32)
    token_scale = 0.3 * jnp.exp(math.log(10.0) * log_level)
    channel_scale = jnp.exp(jax.random.uniform(subkeys[3], (C, 1), jnp.float32, math.log(0.7), math.log(1.4)))
    latent_field = base_noise * token_scale[None, :] * channel_scale
    return latent_field.astype(jnp.bfloat16)


def attention_weights(key):
    subkeys = jax.random.split(jax.random.fold_in(key, 101), 4)
    scale = C ** (-0.5)
    query_w = jnp.clip(jax.random.normal(subkeys[0], (C, C), jnp.float32), -4.0, 4.0) * (1.6 * scale)
    key_w = jnp.clip(jax.random.normal(subkeys[2], (C, C), jnp.float32), -4.0, 4.0) * (1.6 * scale)
    value_w = jnp.clip(jax.random.normal(subkeys[3], (C, C), jnp.float32), -4.0, 4.0) * (3.0 * scale)
    return (query_w, jnp.stack([key_w, value_w]))


def draw_q_w(key, part):
    return attention_weights(key)[0].astype(jnp.bfloat16)


def draw_kv_w(key, part):
    return attention_weights(key)[1].astype(jnp.bfloat16)


def level_of(key, dims, cuts, least, high):
    gain, own = 1.0, jax.random.fold_in(key, 6)
    for position, parts in cuts:
        steps = jnp.exp(jax.random.uniform(jax.random.fold_in(own, position), (parts,), jnp.float32, least / len(cuts), high / len(cuts)))
        gain = gain * jnp.repeat(steps, dims[position] // parts).reshape([-1 if axis == position else 1 for axis in range(len(dims))])
    return gain


def scatter_about(stream_key, extent, width, reach, cuts=(), kind=jnp.bfloat16):
    array = jax.random.normal(stream_key, extent, jnp.float32) * width
    if len(cuts) > 0:
        array = level_of(stream_key, extent, cuts, -0.22, 0.18) * array
    return jnp.clip(array, min=-reach, max=reach).astype(kind)


def setup_inputs(seed: int = 0, part: int = 0) -> dict:
    key_of = jax.random.split(jax.random.key(seed), 12)
    part_splits = jax.random.split(jax.random.fold_in(key_of[11], part), 12)
    return {
        "latent": draw_latent(jax.random.fold_in(jax.random.fold_in(key_of[11], part), 71), part),
        "timestep": jax.random.randint(part_splits[1], (1,), 0, 1000).astype(jnp.int32),
        "time_w1": scatter_about(key_of[2], (TEMB, FREQ), FREQ ** -0.5, 0.3125),
        "time_proj": scatter_about(key_of[3], (C, TEMB), TEMB ** -0.5, 0.15625, ((0, 4),)),
        "conv1_w": scatter_about(key_of[4], (9, C, C), (9 * C) ** -0.5, 0.078125, ((1, 4),)),
        "conv2_w": scatter_about(key_of[5], (9, C, C), (9 * C) ** -0.5, 0.078125, ((1, 4),)),
        "proj_in_w": scatter_about(key_of[6], (C, C), C ** -0.5, 0.25, ((0, 4),)),
        "q_w": draw_q_w(jax.random.fold_in(key_of[11], 71), part),
        "kv_w": draw_kv_w(jax.random.fold_in(key_of[11], 71), part),
        "out_w": scatter_about(key_of[9], (C, C), C ** -0.5, 0.25, ((0, 4),)),
        "proj_out_w": scatter_about(key_of[10], (C, C), C ** -0.5, 0.25, ((0, 4),)),
    }


def rounded(values):
    return lax.optimization_barrier(values.astype(jnp.bfloat16)).astype(jnp.float32)

def group_norm(values, epsilon):
    grouped = values.reshape(NGROUPS, C // NGROUPS, -1)
    centre = lax.optimization_barrier(jnp.mean(grouped, axis=(1, 2), keepdims=True))
    spread = lax.optimization_barrier(jnp.mean((grouped - centre) * (grouped - centre), axis=(1, 2), keepdims=True))
    return ((grouped - centre) / jnp.sqrt(spread + epsilon)).reshape(C, -1)

def convolve(active, weight):
    height = TOKENS // WIDTH
    padded = jnp.pad(active.reshape(C, height, WIDTH), ((0, 0), (1, 1), (1, 1)))
    running = jnp.zeros((C, TOKENS), jnp.float32)
    for offset in range(9):
        row_step, col_step = divmod(offset, 3)
        window = padded[:, row_step:row_step + height, col_step:col_step + WIDTH].reshape(C, TOKENS)
        running = running + jnp.dot(weight[offset], window, preferred_element_type=jnp.float32)
    return running

def time_bias_of(timestep, time_w1, time_proj):
    half_width = FREQ // 2
    frequency = jnp.exp(-math.log(10000.0) * jnp.arange(half_width, dtype=jnp.float32) / half_width)
    angles = timestep[0].astype(jnp.float32) * frequency
    embedded = jnp.concatenate([jnp.cos(angles), jnp.sin(angles)]).astype(jnp.bfloat16)
    hidden = jax.nn.silu(jnp.dot(time_w1, embedded, preferred_element_type=jnp.float32))
    return jnp.dot(time_proj, jax.nn.silu(hidden).astype(jnp.bfloat16), preferred_element_type=jnp.float32)

def attention(layer_normed, q_w, kv_w):
    queries = jnp.dot(q_w, layer_normed, preferred_element_type=jnp.float32) * 0.125
    key_heads = rounded(jnp.dot(kv_w[0], layer_normed, preferred_element_type=jnp.float32)).reshape(HEADS, HEAD_DIM, TOKENS)
    value_heads = rounded(jnp.dot(kv_w[1], layer_normed, preferred_element_type=jnp.float32)).reshape(HEADS, HEAD_DIM, TOKENS)
    block_size = math.gcd(TOKENS, 512)
    block_count = TOKENS // block_size
    query_blocks = rounded(queries).reshape(HEADS, HEAD_DIM, block_count, block_size).transpose(2, 0, 1, 3)

    def one_block(query_block):
        scores = jnp.einsum('hdk,hdb->hkb', key_heads, query_block, precision=lax.Precision.HIGHEST)
        row_peak = lax.optimization_barrier(jnp.max(scores, axis=1, keepdims=True))
        weights = jnp.exp(scores - row_peak)
        row_total = lax.optimization_barrier(jnp.sum(weights, axis=1))
        weighted = jnp.einsum('hdk,hkb->hdb', value_heads, rounded(weights), precision=lax.Precision.HIGHEST)
        return (weighted / row_total[:, None, :]).astype(jnp.bfloat16)
    blocks = lax.map(one_block, query_blocks)
    return blocks.transpose(1, 2, 0, 3).reshape(C, TOKENS)

def reference(latent, timestep, time_w1, time_proj, conv1_w, conv2_w, proj_in_w, q_w, kv_w, out_w, proj_out_w):
    latent_f32 = latent.astype(jnp.float32)
    time_bias = time_bias_of(timestep, time_w1, time_proj)
    act_one = jax.nn.silu(group_norm(latent_f32, 1e-05)).astype(jnp.bfloat16)
    conv_one = (convolve(act_one, conv1_w) + time_bias[:, None]).astype(jnp.bfloat16)
    act_two = jax.nn.silu(group_norm(conv_one.astype(jnp.float32), 1e-05)).astype(jnp.bfloat16)
    resnet = (latent_f32 + convolve(act_two, conv2_w)).astype(jnp.bfloat16)
    normed = group_norm(resnet.astype(jnp.float32), 1e-06).astype(jnp.bfloat16)
    projected = jnp.dot(proj_in_w, normed, preferred_element_type=jnp.float32).astype(jnp.bfloat16)
    proj_f32 = projected.astype(jnp.float32)
    centre = lax.optimization_barrier(jnp.mean(proj_f32, axis=0, keepdims=True))
    spread = lax.optimization_barrier(jnp.mean((proj_f32 - centre) * (proj_f32 - centre), axis=0, keepdims=True))
    layer_normed = ((proj_f32 - centre) / jnp.sqrt(spread + 1e-05)).astype(jnp.bfloat16)
    attended = attention(layer_normed, q_w, kv_w)
    mixed = (proj_f32 + jnp.dot(out_w, attended, preferred_element_type=jnp.float32)).astype(jnp.bfloat16)
    return (resnet.astype(jnp.float32) + jnp.dot(proj_out_w, mixed, preferred_element_type=jnp.float32)).astype(jnp.bfloat16)
```

```python
import math

import jax
import jax.numpy as jnp
from jax import lax
from jax.sharding import PartitionSpec as P

C = 640
HEADS = 10
HEAD_DIM = 64
NGROUPS = 32
FREQ = 320
WIDTH = 256
BF16 = jnp.bfloat16
F32 = jnp.float32


def moved(array, axis, by):
    count = lax.axis_size(axis)
    return lax.ppermute(array, axis, [(i, (i + by) % count) for i in range(count)])


def gathered_rows(own):
    channels, band_len = own.shape
    height = band_len // WIDTH
    count = lax.axis_size("patch")
    own_rows = own.reshape(channels, height, WIDTH).transpose(1, 0, 2)
    if count > 4:
        return lax.all_gather(own_rows, "patch", axis=0, tiled=True)
    position = lax.axis_index("patch")
    arrived = [own_rows] + [moved(own_rows, "patch", by) for by in range(1, count)]
    rows = jnp.zeros((count * height, channels, WIDTH), own.dtype)
    for by, part in enumerate(arrived):
        rows = lax.dynamic_update_slice(rows, part, ((position - by) % count * height, 0, 0))
    return rows


def gathered_over(array, axis, dim):
    count = lax.axis_size(axis)
    if count != 2:
        return lax.all_gather(array, axis, axis=dim, tiled=True)
    other = moved(array, axis, 1)
    first = lax.axis_index(axis) == 0
    return jnp.concatenate(
        [jnp.where(first, array, other), jnp.where(first, other, array)], axis=dim
    )


def gathered_channels(array, dim):
    shape = array.shape
    own = lax.expand_dims(array, (dim,))
    both = gathered_over(own, "chan", dim)
    both = lax.expand_dims(both, (dim + 1,))
    every = gathered_over(both, "sub", dim + 1)
    return every.reshape(shape[:dim] + (-1,) + shape[dim + 1 :])


def group_norm(values, epsilon):
    rows, channels, width = values.shape
    group_size = C // NGROUPS
    cell_count = group_size * rows * width

    def per_channel(sums):
        groups = jnp.sum(sums.reshape(channels // group_size, group_size), axis=1) / cell_count
        return jnp.repeat(groups, group_size)[None, :, None]

    centre = per_channel(jnp.sum(values, axis=(0, 2)))
    shifted = values - centre
    spread = per_channel(jnp.sum(shifted * shifted, axis=(0, 2)))
    return shifted * lax.rsqrt(spread + epsilon)


def convolve(active, weight):
    rows = active.shape[0]
    padded = jnp.pad(active, ((1, 1), (0, 0), (1, 1)))
    running = None
    for offset in range(9):
        row_step, col_step = divmod(offset, 3)
        window = padded[row_step : row_step + rows, :, col_step : col_step + WIDTH]
        term = jnp.einsum("oc,rcx->rox", weight[offset], window, preferred_element_type=F32)
        running = term if running is None else running + term
    return running


def time_bias_of(timestep, time_w1, time_proj):
    half_width = FREQ // 2
    frequency = jnp.exp(-math.log(10000.0) * jnp.arange(half_width, dtype=F32) / half_width)
    angles = timestep[0].astype(F32) * frequency
    embedded = jnp.concatenate([jnp.cos(angles), jnp.sin(angles)]).astype(BF16)
    time_hidden = jax.nn.silu(jnp.dot(time_w1, embedded, preferred_element_type=F32))
    return jnp.dot(time_proj, jax.nn.silu(time_hidden).astype(BF16), preferred_element_type=F32)


def local(
    latent, timestep, time_w1, time_proj, conv1_w, conv2_w, proj_in_w, q_w, kv_w, out_w, proj_out_w
):
    band_len = latent.shape[1]
    height = band_len // WIDTH
    position = lax.axis_index("patch")
    chan_count, sub_count = lax.axis_size("chan"), lax.axis_size("sub")
    by_heads = HEADS % chan_count == 0

    latent_rows = gathered_rows(latent)
    time_bias = time_bias_of(timestep, time_w1, time_proj)
    proj_in_all = gathered_channels(proj_in_w, 0)
    out_all = gathered_channels(out_w, 0)
    qkv_own = jnp.concatenate([q_w[None], kv_w], axis=0)
    if by_heads:
        qkv_w = gathered_over(qkv_own, "sub", 1)
    else:
        qkv_w = gathered_channels(qkv_own, 1)

    latent_f32 = latent_rows.astype(F32)
    act_one = jax.nn.silu(group_norm(latent_f32, 1e-05)).astype(BF16)
    conv_one = (
        convolve(gathered_channels(act_one, 1), conv1_w) + time_bias[None, :, None]
    ).astype(BF16)
    act_two = jax.nn.silu(group_norm(conv_one.astype(F32), 1e-05)).astype(BF16)
    resnet = (latent_f32 + convolve(gathered_channels(act_two, 1), conv2_w)).astype(BF16)
    normed = group_norm(resnet.astype(F32), 1e-06).astype(BF16)
    normed_all = gathered_channels(normed, 1)
    projected = jnp.einsum(
        "oc,rcx->rox", proj_in_all, normed_all, preferred_element_type=F32
    ).astype(BF16)
    proj_f32 = projected.astype(F32)
    centre = jnp.mean(proj_f32, axis=1, keepdims=True)
    spread = jnp.mean((proj_f32 - centre) * (proj_f32 - centre), axis=1, keepdims=True)
    layer_normed = ((proj_f32 - centre) * lax.rsqrt(spread + 1e-05)).astype(BF16)
    key_value = jnp.einsum(
        "joc,rcx->jrox", qkv_w[1:], layer_normed, preferred_element_type=F32
    ).astype(BF16)
    splits = sub_count if by_heads else sub_count * chan_count
    slot = lax.axis_index("sub") if by_heads else lax.axis_index("chan") * sub_count + lax.axis_index("sub")
    share = WIDTH // splits
    band_rows = lambda array: lax.dynamic_slice_in_dim(array, position * height, height, axis=0)
    mine = lax.dynamic_slice_in_dim(band_rows(layer_normed), slot * share, share, axis=2)
    query = (
        jnp.einsum("oc,rcx->rox", qkv_w[0], mine, preferred_element_type=F32) * 0.125
    ).astype(BF16)
    heads = query.shape[1] // HEAD_DIM
    rows = projected.shape[0]
    query = query.reshape(height, heads, HEAD_DIM, share)
    keys = key_value[0].reshape(rows, heads, HEAD_DIM, WIDTH)
    values = key_value[1].reshape(rows, heads, HEAD_DIM, WIDTH)
    scores = jnp.einsum("rhdk,qhdb->hrkqb", keys, query, preferred_element_type=F32)
    peak = jnp.max(scores, axis=(1, 2), keepdims=True)
    weights = jnp.exp(scores - peak)
    total = jnp.sum(weights, axis=(1, 2))
    weighted = jnp.einsum(
        "rhdk,hrkqb->hdqb", values, weights.astype(BF16), preferred_element_type=F32
    )
    attended = (weighted / total[:, None]).astype(BF16)
    attended = attended.reshape(heads * HEAD_DIM, height, share).transpose(1, 0, 2)
    if by_heads:
        attended = gathered_over(gathered_over(attended, "chan", 1), "sub", 2)
    else:
        attended = lax.all_gather(attended, ("chan", "sub"), axis=2, tiled=True)
    mixed = (
        band_rows(proj_f32)
        + jnp.einsum("oc,rcx->rox", out_all, attended, preferred_element_type=F32)
    ).astype(BF16)
    final = band_rows(resnet).astype(F32) + jnp.einsum(
        "oc,rcx->rox", proj_out_w, mixed, preferred_element_type=F32
    )
    return final.astype(BF16).transpose(1, 0, 2).reshape(latent.shape)


def banded_with_halo(cells, sides, width):
    for axis, dim in sides:
        count = lax.axis_size(axis)
        ends = count - 1
        head = lax.slice_in_dim(cells, 0, width, axis=dim)
        tail = lax.slice_in_dim(cells, cells.shape[dim] - width, cells.shape[dim], axis=dim)
        cells = jnp.concatenate(
            [
                lax.ppermute(tail, axis, [(i, (i + 1) % count) for i in range(ends)]),
                cells,
                lax.ppermute(head, axis, [((i + 1) % count, i) for i in range(ends)]),
            ],
            axis=dim,
        )
    return cells


def banded_from_behind(array, axis, by):
    count = lax.axis_size(axis)
    return lax.ppermute(array, axis, [(i, (i + by) % count) for i in range(count)])


def banded_merged(array, axis, combine):
    everything = jax.tree.map(lambda part: lax.all_gather(part, axis), array)
    first = jax.tree.map(lambda part: part[0], everything)

    def turn(k, so_far):
        return combine(so_far, jax.tree.map(lambda part: part[k], everything))

    return lax.fori_loop(1, lax.axis_size(axis), turn, first)


def banded_group_norm(values, epsilon):
    channels, band_len = values.shape
    group_size = C // NGROUPS
    grouped = values.reshape(channels // group_size, group_size, band_len)
    cell_count = group_size * band_len * lax.axis_size("patch")
    centre = lax.psum(jnp.sum(grouped, axis=(1, 2)), "patch") / cell_count
    shifted = grouped - centre[:, None, None]
    spread = lax.psum(jnp.sum(shifted * shifted, axis=(1, 2)), "patch") / cell_count
    normal_form = (grouped - centre[:, None, None]) * lax.rsqrt(spread + epsilon)[:, None, None]
    return normal_form.reshape(channels, band_len)


def banded_convolve(active, weight):
    own_channels, band_len = active.shape
    height = band_len // WIDTH
    whole_rows = lax.all_gather(active, ("chan", "sub"), axis=0, tiled=True)
    image_grid = whole_rows.reshape(whole_rows.shape[0], height, WIDTH)
    padded = banded_with_halo(image_grid, (("patch", 1),), 1)
    channels = padded.shape[0]
    padded = jnp.pad(padded, ((0, 0), (0, 0), (1, 1)))
    running = jnp.zeros((weight.shape[1], band_len), jnp.float32)
    for offset in range(9):
        row_step, col_step = divmod(offset, 3)
        window = padded[:, row_step : row_step + height, col_step : col_step + WIDTH].reshape(
            channels, band_len
        )
        running = running + jnp.dot(weight[offset], window, preferred_element_type=jnp.float32)
    return running


def banded_combine_parts(earlier_part, later_part):
    peak_one, total_one, sums_one = earlier_part
    peak_two, total_two, sums_two = later_part
    new_peak = jnp.maximum(peak_one, peak_two)
    factor_one = jnp.exp(peak_one - new_peak)
    factor_two = jnp.exp(peak_two - new_peak)
    new_total = total_one * factor_one + total_two * factor_two
    new_sums = sums_one * factor_one[:, None, :] + sums_two * factor_two[:, None, :]
    return (new_peak, new_total, new_sums)


def banded_advance(kv_piece):
    return banded_from_behind(kv_piece, "patch", 1)


def banded(
    latent, timestep, time_w1, time_proj, conv1_w, conv2_w, proj_in_w, q_w, kv_w, out_w, proj_out_w
):
    latent_f32 = latent.astype(jnp.float32)
    band_len = latent.shape[1]
    half_width = FREQ // 2
    frequency = jnp.exp(-math.log(10000.0) * jnp.arange(half_width, dtype=jnp.float32) / half_width)
    angles = timestep[0].astype(jnp.float32) * frequency
    embedded = jnp.concatenate([jnp.cos(angles), jnp.sin(angles)]).astype(jnp.bfloat16)
    time_hidden = jax.nn.silu(jnp.dot(time_w1, embedded, preferred_element_type=jnp.float32))
    time_bias = jnp.dot(
        time_proj, jax.nn.silu(time_hidden).astype(jnp.bfloat16), preferred_element_type=jnp.float32
    )
    act_one = jax.nn.silu(banded_group_norm(latent_f32, 1e-05)).astype(jnp.bfloat16)
    conv_one = (banded_convolve(act_one, conv1_w) + time_bias[:, None]).astype(jnp.bfloat16)
    act_two = jax.nn.silu(banded_group_norm(conv_one.astype(jnp.float32), 1e-05)).astype(jnp.bfloat16)
    resnet = (latent_f32 + banded_convolve(act_two, conv2_w)).astype(jnp.bfloat16)
    normed = banded_group_norm(resnet.astype(jnp.float32), 1e-06).astype(jnp.bfloat16)
    columns = proj_in_w
    projected = jnp.dot(
        columns,
        lax.all_gather(normed, ("chan", "sub"), axis=0, tiled=True),
        preferred_element_type=jnp.float32,
    ).astype(jnp.bfloat16)
    whole_proj = lax.all_gather(projected, ("chan", "sub"), axis=0, tiled=True).astype(jnp.float32)
    centre = jnp.mean(whole_proj, axis=0, keepdims=True)
    spread = jnp.mean((whole_proj - centre) * (whole_proj - centre), axis=0, keepdims=True)
    layer_normed = ((whole_proj - centre) / jnp.sqrt(spread + 1e-05)).astype(jnp.bfloat16)
    query_own = (jnp.dot(q_w, layer_normed, preferred_element_type=jnp.float32) * 0.125).astype(
        jnp.bfloat16
    )
    queries = lax.all_gather(query_own, ("chan", "sub"), axis=0, tiled=True).reshape(
        HEADS, HEAD_DIM, band_len
    )
    key_value = jnp.einsum(
        "joc,cb->jbo", kv_w, layer_normed, preferred_element_type=jnp.float32
    ).astype(jnp.bfloat16)
    slot_pairs = lax.all_to_all(key_value, ("chan", "sub"), split_axis=1, concat_axis=2, tiled=True)

    def attend(softmax_state, kv_piece):
        row_peak, row_total, weighted = softmax_state
        slot_len = kv_piece.shape[1]
        key_heads = kv_piece[0].reshape(slot_len, HEADS, HEAD_DIM)
        value_heads = kv_piece[1].reshape(slot_len, HEADS, HEAD_DIM)
        scores = jnp.einsum("khd,hdb->hkb", key_heads, queries, preferred_element_type=jnp.float32)
        new_peak = jnp.maximum(row_peak, jnp.max(scores, axis=1))
        factor = jnp.exp(row_peak - new_peak)
        weights = jnp.exp(scores - new_peak[:, None, :])
        new_total = row_total * factor + jnp.sum(weights, axis=1)
        update = jnp.einsum(
            "khd,hkb->hdb",
            value_heads,
            weights.astype(jnp.bfloat16),
            preferred_element_type=jnp.float32,
        )
        return (new_peak, new_total, weighted * factor[:, None, :] + update)

    start_state = (
        jnp.full((HEADS, band_len), -1e30, jnp.float32),
        jnp.zeros((HEADS, band_len), jnp.float32),
        jnp.zeros((HEADS, HEAD_DIM, band_len), jnp.float32),
    )
    softmax_state = attend(start_state, slot_pairs)
    band_count = lax.axis_size("patch")

    def one_side(step_index, packed):
        state_now, ahead = packed
        ahead = banded_advance(ahead)
        return (attend(state_now, ahead), ahead)

    softmax_state, ahead = lax.fori_loop(0, band_count - 1, one_side, (softmax_state, slot_pairs))
    row_peak, row_total, weighted = banded_merged(softmax_state, ("chan", "sub"), banded_combine_parts)
    attended = (
        (weighted / row_total[:, None, :]).reshape(HEADS * HEAD_DIM, band_len).astype(jnp.bfloat16)
    )
    mixed = (
        projected.astype(jnp.float32) + jnp.dot(out_w, attended, preferred_element_type=jnp.float32)
    ).astype(jnp.bfloat16)
    columns = proj_out_w
    final_sum = resnet.astype(jnp.float32) + jnp.dot(
        columns,
        lax.all_gather(mixed, ("chan", "sub"), axis=0, tiled=True),
        preferred_element_type=jnp.float32,
    )
    return final_sum.astype(jnp.bfloat16)


def solution(mesh):
    in_specs = (
        P(("chan", "sub"), ("groups", "patch")),
        P("groups"),
        P(),
        P(("chan", "sub"), None),
        P(None, ("chan", "sub"), None),
        P(None, ("chan", "sub"), None),
        P(("chan", "sub"), None),
        P(("chan", "sub"), None),
        P(None, ("chan", "sub"), None),
        P(("chan", "sub"), None),
        P(("chan", "sub"), None),
    )
    out_specs = P(("chan", "sub"), ("groups", "patch"))
    small = mesh.shape["patch"] <= 4 and mesh.shape["chan"] == 2 and mesh.shape["sub"] == 2
    plan = local if small else banded
    return jax.shard_map(plan, mesh=mesh, in_specs=in_specs, out_specs=out_specs, check_vma=False)
```

```python
import math

import jax
import jax.numpy as jnp
from jax import lax
from jax.experimental import pallas as pl
from jax.experimental.pallas import tpu as pltpu
from jax.sharding import PartitionSpec as P

C = 640
HEADS = 10
HEAD_DIM = 64
NGROUPS = 32
GROUP = C // NGROUPS
FREQ = 320
WIDTH = 256
BF16 = jnp.bfloat16
F32 = jnp.float32

OWN = C // 4
CHUNK = OWN // 2
FLIPS = (0, 2, 1, 3)


def call(kernel, outs, *args, scratch=(), flops=0, limit=24):
    specs = [pl.BlockSpec(memory_space=pltpu.SMEM)]
    specs += [pl.BlockSpec(memory_space=pltpu.VMEM)] * (len(args) - 1)
    moved = sum(math.prod(a.shape) * a.dtype.itemsize for a in args)
    return pl.pallas_call(
        kernel,
        out_shape=[jax.ShapeDtypeStruct(s, t) for s, t in outs],
        in_specs=specs,
        out_specs=[pl.BlockSpec(memory_space=pltpu.VMEM)] * len(outs),
        scratch_shapes=[pltpu.VMEM(s, t) for s, t in scratch],
        compiler_params=pltpu.CompilerParams(vmem_limit_bytes=limit << 20),
        cost_estimate=pl.CostEstimate(flops=flops, transcendentals=0, bytes_accessed=moved),
    )(*args)


def group_sums(sums):
    wide = jnp.broadcast_to(sums, (sums.shape[0], 128))
    row = lax.broadcasted_iota(jnp.int32, wide.shape, 0)
    result = jnp.zeros_like(wide)
    for start in range(0, wide.shape[0], GROUP):
        inside = (row >= start) & (row < start + GROUP)
        total = jnp.sum(jnp.where(inside, wide, 0.0), axis=0, keepdims=True)
        result = jnp.where(inside, total, result)
    return result[:, :1]


def normal_form(rows, epsilon):
    cell_count = GROUP * len(rows) * rows[0].shape[1]
    centre = group_sums(sum(jnp.sum(row, axis=1, keepdims=True) for row in rows)) / cell_count
    shifted = [row - centre for row in rows]
    spread = group_sums(sum(jnp.sum(row * row, axis=1, keepdims=True) for row in shifted))
    scale = lax.rsqrt(spread / cell_count + epsilon)
    return [row * scale for row in shifted]


def silu(values):
    return values * jax.nn.sigmoid(values)


def first_norm(ids, *refs):
    count = (len(refs) - 3)
    pieces, (rows_ref, one_ref, two_ref) = refs[:count], refs[count:]
    places = [lax.rem(ids[0] + count - by, count) for by in range(count)]
    for piece, place in zip(pieces, places):
        rows_ref[place] = piece[...]
    for part, out in enumerate((one_ref, two_ref)):
        values = [piece[part * CHUNK : (part + 1) * CHUNK, :].astype(F32) for piece in pieces]
        for value, place in zip(normal_form(values, 1e-05), places):
            out[place] = silu(value).astype(BF16)


def arrange(ids, weight, one_ref, two_ref):
    for tap in range(9):
        i, j = divmod(tap, 3)
        for part in range(2):
            source = weight[tap, part * CHUNK : (part + 1) * CHUNK, :]
            for block in range(4):
                for half, out in enumerate((one_ref, two_ref)):
                    at = block * OWN + half * CHUNK
                    to = (i * 4 + block) * CHUNK
                    row = (part * 3 + j) * CHUNK
                    out[row : row + CHUNK, to : to + CHUNK] = source[:, at : at + CHUNK]


def place_blocks(ids, blocks, padded):
    rows = blocks[0].shape[0]
    edge = jnp.zeros(padded.shape[1:], padded.dtype)
    padded[0] = edge
    padded[rows + 1] = edge
    for flip, block in zip(FLIPS, blocks):
        at = pl.multiple_of((ids[1] ^ flip) * CHUNK, 16)
        padded[1 : rows + 1, pl.ds(at, CHUNK), :] = block[...]


def taps(weight, padded, row):
    window = padded[row : row + 3].reshape(3 * 4 * CHUNK, WIDTH)
    every = jnp.dot(weight[...], window, preferred_element_type=F32)
    lane = lax.broadcasted_iota(jnp.int32, (CHUNK, WIDTH), 1)
    results = []
    for start in range(0, every.shape[0], 3 * CHUNK):
        left, here, right = (
            every[start + j * CHUNK : start + (j + 1) * CHUNK] for j in range(3)
        )
        left = jnp.where(lane == 0, 0.0, pltpu.roll(left, 1, 1))
        right = jnp.where(lane == WIDTH - 1, 0.0, pltpu.roll(right, WIDTH - 1, 1))
        results.append(here + left + right)
    return results


def half_conv(ids, own, chan, sub, both, weight, one_ref, two_ref, padded):
    place_blocks(ids, (own, chan, sub, both), padded)
    for row in range(own.shape[0]):
        one_ref[row], two_ref[row] = taps(weight, padded, row)


def first_conv(ids, own, chan, sub, both, weight, half, bias, act_ref, padded):
    place_blocks(ids, (own, chan, sub, both), padded)
    rows = []
    for row in range(own.shape[0]):
        (rest,) = taps(weight, padded, row)
        rows.append((half[row] + rest + bias[...]).astype(BF16).astype(F32))
    for row, value in enumerate(normal_form(rows, 1e-05)):
        act_ref[row] = silu(value).astype(BF16)


def second_conv(part):
    def kernel(ids, own, chan, sub, both, weight, half, latent, act_ref, resnet_ref, padded, sums):
        place_blocks(ids, (own, chan, sub, both), padded)
        rows = []
        for row in range(own.shape[0]):
            (rest,) = taps(weight, padded, row)
            value = latent[row, part * CHUNK : (part + 1) * CHUNK, :].astype(F32) + (half[row] + rest)
            value = value.astype(BF16)
            sums[row] = value
            rows.append(value.astype(F32))
        resnet_ref[...] = sums[ids[0]]
        for row, value in enumerate(normal_form(rows, 1e-06)):
            act_ref[row] = value.astype(BF16)

    return kernel


def stack_rows(ids, own, chan, sub, both, full):
    for flip, block in zip(FLIPS, (own, chan, sub, both)):
        full[pl.ds(pl.multiple_of((ids[1] ^ flip) * OWN, 16), OWN), :] = block[...]


def stack_heads(ids, q_own, kv_own, q_sub, kv_sub, q_ref, k_ref, v_ref):
    here = pl.multiple_of(ids[2] * OWN, 16)
    there = pl.multiple_of((1 - ids[2]) * OWN, 16)
    for at, q_part, kv_part in ((here, q_own, kv_own), (there, q_sub, kv_sub)):
        q_ref[pl.ds(at, OWN), :] = q_part[...]
        k_ref[pl.ds(at, OWN), :] = kv_part[0]
        v_ref[pl.ds(at, OWN), :] = kv_part[1]


def attend(ids, *refs):
    blocks, refs = refs[:8], refs[8:]
    proj_w, q_w, k_w, v_w, out_ref, proj_ref, normed, projected, layered, keys, values = refs
    rows = normed.shape[0]
    for half in range(2):
        for flip, block in zip(FLIPS, blocks[half * 4 : half * 4 + 4]):
            at = pl.multiple_of((ids[1] ^ flip) * OWN + half * CHUNK, 16)
            normed[:, pl.ds(at, CHUNK), :] = block[...]
    for row in range(rows):
        value = jnp.dot(proj_w[...], normed[row], preferred_element_type=F32).astype(BF16)
        projected[row] = value
        value = value.astype(F32)
        shifted = value - jnp.sum(value, axis=0, keepdims=True) / C
        spread = jnp.sum(shifted * shifted, axis=0, keepdims=True) / C
        layer = (shifted * lax.rsqrt(spread + 1e-05)).astype(BF16)
        layered[row] = layer
        at = slice(row * WIDTH, (row + 1) * WIDTH)
        keys[:, at] = jnp.dot(k_w[...], layer, preferred_element_type=F32).astype(BF16)
        values[:, at] = jnp.dot(v_w[...], layer, preferred_element_type=F32).astype(BF16)
    proj_ref[...] = projected[ids[0]]
    share = out_ref.shape[1]
    mine = layered[ids[0], :, pl.ds(pl.multiple_of(ids[2] * share, 128), share)]
    query = (jnp.dot(q_w[...], mine, preferred_element_type=F32) * 0.125).astype(BF16)
    for head in range(query.shape[0] // HEAD_DIM):
        at = slice(head * HEAD_DIM, (head + 1) * HEAD_DIM)
        scores = lax.dot_general(
            keys[at, :], query[at], (((0,), (0,)), ((), ())), preferred_element_type=F32
        )
        weights = jnp.exp(scores - jnp.max(scores, axis=0, keepdims=True))
        total = jnp.sum(weights, axis=0, keepdims=True)
        weighted = jnp.dot(values[at, :], weights.astype(BF16), preferred_element_type=F32)
        out_ref[at, :] = (weighted / total).astype(BF16)


def finish(ids, own, chan, sub, both, proj, res_one, res_two, out_w, last_w, out_ref, attended):
    channels, share = own.shape
    for flip, block in zip(FLIPS, (own, chan, sub, both)):
        place = ids[1] ^ flip
        at = pl.multiple_of((place >> 1) * channels, 16)
        lanes = pl.multiple_of((place & 1) * share, 128)
        attended[pl.ds(at, channels), pl.ds(lanes, share)] = block[...]
    mixed = proj[...].astype(F32) + jnp.dot(
        out_w[...], attended[...], preferred_element_type=F32
    )
    last = jnp.dot(last_w[...], mixed.astype(BF16), preferred_element_type=F32)
    for part, res in enumerate((res_one, res_two)):
        at = slice(part * CHUNK, (part + 1) * CHUNK)
        out_ref[at, :] = (res[...].astype(F32) + last[at]).astype(BF16)


def swapped(array, axis):
    return lax.ppermute(array, axis, [(0, 1), (1, 0)])


def exchanged(own):
    chan = swapped(own, "chan")
    return own, chan, swapped(own, "sub"), swapped(chan, "sub")


def time_bias_of(timestep, time_w1, time_proj):
    half_width = FREQ // 2
    frequency = jnp.exp(-math.log(10000.0) * jnp.arange(half_width, dtype=F32) / half_width)
    angles = timestep[0].astype(F32) * frequency
    embedded = jnp.concatenate([jnp.cos(angles), jnp.sin(angles)]).astype(BF16)
    time_hidden = jax.nn.silu(jnp.dot(time_w1, embedded, preferred_element_type=F32))
    return jnp.dot(time_proj, jax.nn.silu(time_hidden).astype(BF16), preferred_element_type=F32)


def whole_rows(
    latent, timestep, time_w1, time_proj, conv1_w, conv2_w, proj_in_w, q_w, kv_w, out_w, proj_out_w
):
    rows = lax.axis_size("patch")
    sub = lax.axis_index("sub")
    ids = jnp.stack([lax.axis_index("patch"), lax.axis_index("chan") * 2 + sub, sub])
    pieces = [latent] + [
        lax.ppermute(latent, "patch", [(i, (i + by) % rows) for i in range(rows)])
        for by in range(1, rows)
    ]
    chunk = (rows, CHUNK, WIDTH)
    padded = ((rows + 2, 4 * CHUNK, WIDTH), BF16)
    tap_flops = 2 * 3 * CHUNK * 12 * CHUNK * rows * WIDTH

    def arranged(weight):
        return call(arrange, [((6 * CHUNK, 12 * CHUNK), BF16)] * 2, ids, weight, flops=10**9)

    conv1_one, conv1_two = arranged(conv1_w)
    conv2_one, conv2_two = arranged(conv2_w)
    bias = time_bias_of(timestep, time_w1, time_proj).reshape(2, CHUNK, 1)

    def stacked(weight):
        return call(stack_rows, [((C, C), BF16)], ids, *exchanged(weight), flops=10**8)[0]

    proj_in_all = stacked(proj_in_w)
    out_all = stacked(out_w)
    heads_w = call(
        stack_heads, [((2 * OWN, C), BF16)] * 3,
        ids, q_w, kv_w, swapped(q_w, "sub"), swapped(kv_w, "sub"), flops=10**8,
    )

    latent_rows, one, two = call(
        first_norm, [((rows, OWN, WIDTH), BF16), (chunk, BF16), (chunk, BF16)], ids, *pieces
    )

    def halves(one, weight):
        return call(
            half_conv, [(chunk, F32)] * 2, ids, *exchanged(one), weight,
            scratch=[padded], flops=2 * tap_flops,
        )

    out_part = lambda weight, part: weight[part * 3 * CHUNK : (part + 1) * 3 * CHUNK]
    half = halves(one, conv1_one)
    blocks = exchanged(two)
    one, two = (
        call(
            first_conv, [(chunk, BF16)], ids, *blocks, out_part(conv1_two, part), half[part],
            bias[part], scratch=[padded], flops=tap_flops,
        )[0]
        for part in range(2)
    )
    half = halves(one, conv2_one)
    blocks = exchanged(two)
    (one, res_one), (two, res_two) = (
        call(
            second_conv(part), [(chunk, BF16), ((CHUNK, WIDTH), BF16)],
            ids, *blocks, out_part(conv2_two, part), half[part], latent_rows,
            scratch=[padded, (chunk, BF16)], flops=tap_flops,
        )
        for part in range(2)
    )
    share = WIDTH // 2
    attended, projected = call(
        attend, [((2 * OWN, share), BF16), ((C, WIDTH), BF16)],
        ids, *exchanged(one), *exchanged(two), proj_in_all, *heads_w,
        scratch=[((rows, C, WIDTH), BF16)] * 3 + [((2 * OWN, rows * WIDTH), BF16)] * 2,
        flops=4 * 10**9, limit=32,
    )
    return call(
        finish, [((OWN, WIDTH), BF16)], ids, *exchanged(attended), projected, res_one, res_two,
        out_all, proj_out_w, scratch=[((C, WIDTH), BF16)],
    )[0]


def banded_with_halo(cells, sides, width):
    for axis, dim in sides:
        count = lax.axis_size(axis)
        ends = count - 1
        head = lax.slice_in_dim(cells, 0, width, axis=dim)
        tail = lax.slice_in_dim(cells, cells.shape[dim] - width, cells.shape[dim], axis=dim)
        cells = jnp.concatenate(
            [
                lax.ppermute(tail, axis, [(i, (i + 1) % count) for i in range(ends)]),
                cells,
                lax.ppermute(head, axis, [((i + 1) % count, i) for i in range(ends)]),
            ],
            axis=dim,
        )
    return cells


def banded_from_behind(array, axis, by):
    count = lax.axis_size(axis)
    return lax.ppermute(array, axis, [(i, (i + by) % count) for i in range(count)])


def banded_merged(array, axis, combine):
    everything = jax.tree.map(lambda part: lax.all_gather(part, axis), array)
    first = jax.tree.map(lambda part: part[0], everything)

    def turn(k, so_far):
        return combine(so_far, jax.tree.map(lambda part: part[k], everything))

    return lax.fori_loop(1, lax.axis_size(axis), turn, first)


def banded_group_norm(values, epsilon):
    channels, band_len = values.shape
    group_size = C // NGROUPS
    grouped = values.reshape(channels // group_size, group_size, band_len)
    cell_count = group_size * band_len * lax.axis_size("patch")
    centre = lax.psum(jnp.sum(grouped, axis=(1, 2)), "patch") / cell_count
    shifted = grouped - centre[:, None, None]
    spread = lax.psum(jnp.sum(shifted * shifted, axis=(1, 2)), "patch") / cell_count
    normal_form = (grouped - centre[:, None, None]) * lax.rsqrt(spread + epsilon)[:, None, None]
    return normal_form.reshape(channels, band_len)


def banded_convolve(active, weight):
    own_channels, band_len = active.shape
    height = band_len // WIDTH
    whole_rows = lax.all_gather(active, ("chan", "sub"), axis=0, tiled=True)
    image_grid = whole_rows.reshape(whole_rows.shape[0], height, WIDTH)
    padded = banded_with_halo(image_grid, (("patch", 1),), 1)
    channels = padded.shape[0]
    padded = jnp.pad(padded, ((0, 0), (0, 0), (1, 1)))
    running = jnp.zeros((weight.shape[1], band_len), jnp.float32)
    for offset in range(9):
        row_step, col_step = divmod(offset, 3)
        window = padded[:, row_step : row_step + height, col_step : col_step + WIDTH].reshape(
            channels, band_len
        )
        running = running + jnp.dot(weight[offset], window, preferred_element_type=jnp.float32)
    return running


def banded_combine_parts(earlier_part, later_part):
    peak_one, total_one, sums_one = earlier_part
    peak_two, total_two, sums_two = later_part
    new_peak = jnp.maximum(peak_one, peak_two)
    factor_one = jnp.exp(peak_one - new_peak)
    factor_two = jnp.exp(peak_two - new_peak)
    new_total = total_one * factor_one + total_two * factor_two
    new_sums = sums_one * factor_one[:, None, :] + sums_two * factor_two[:, None, :]
    return (new_peak, new_total, new_sums)


def banded_advance(kv_piece):
    return banded_from_behind(kv_piece, "patch", 1)


def banded(
    latent, timestep, time_w1, time_proj, conv1_w, conv2_w, proj_in_w, q_w, kv_w, out_w, proj_out_w
):
    latent_f32 = latent.astype(jnp.float32)
    band_len = latent.shape[1]
    half_width = FREQ // 2
    frequency = jnp.exp(-math.log(10000.0) * jnp.arange(half_width, dtype=jnp.float32) / half_width)
    angles = timestep[0].astype(jnp.float32) * frequency
    embedded = jnp.concatenate([jnp.cos(angles), jnp.sin(angles)]).astype(jnp.bfloat16)
    time_hidden = jax.nn.silu(jnp.dot(time_w1, embedded, preferred_element_type=jnp.float32))
    time_bias = jnp.dot(
        time_proj, jax.nn.silu(time_hidden).astype(jnp.bfloat16), preferred_element_type=jnp.float32
    )
    act_one = jax.nn.silu(banded_group_norm(latent_f32, 1e-05)).astype(jnp.bfloat16)
    conv_one = (banded_convolve(act_one, conv1_w) + time_bias[:, None]).astype(jnp.bfloat16)
    act_two = jax.nn.silu(banded_group_norm(conv_one.astype(jnp.float32), 1e-05)).astype(jnp.bfloat16)
    resnet = (latent_f32 + banded_convolve(act_two, conv2_w)).astype(jnp.bfloat16)
    normed = banded_group_norm(resnet.astype(jnp.float32), 1e-06).astype(jnp.bfloat16)
    columns = proj_in_w
    projected = jnp.dot(
        columns,
        lax.all_gather(normed, ("chan", "sub"), axis=0, tiled=True),
        preferred_element_type=jnp.float32,
    ).astype(jnp.bfloat16)
    whole_proj = lax.all_gather(projected, ("chan", "sub"), axis=0, tiled=True).astype(jnp.float32)
    centre = jnp.mean(whole_proj, axis=0, keepdims=True)
    spread = jnp.mean((whole_proj - centre) * (whole_proj - centre), axis=0, keepdims=True)
    layer_normed = ((whole_proj - centre) / jnp.sqrt(spread + 1e-05)).astype(jnp.bfloat16)
    query_own = (jnp.dot(q_w, layer_normed, preferred_element_type=jnp.float32) * 0.125).astype(
        jnp.bfloat16
    )
    queries = lax.all_gather(query_own, ("chan", "sub"), axis=0, tiled=True).reshape(
        HEADS, HEAD_DIM, band_len
    )
    key_value = jnp.einsum(
        "joc,cb->jbo", kv_w, layer_normed, preferred_element_type=jnp.float32
    ).astype(jnp.bfloat16)
    slot_pairs = lax.all_to_all(key_value, ("chan", "sub"), split_axis=1, concat_axis=2, tiled=True)

    def attend(softmax_state, kv_piece):
        row_peak, row_total, weighted = softmax_state
        slot_len = kv_piece.shape[1]
        key_heads = kv_piece[0].reshape(slot_len, HEADS, HEAD_DIM)
        value_heads = kv_piece[1].reshape(slot_len, HEADS, HEAD_DIM)
        scores = jnp.einsum("khd,hdb->hkb", key_heads, queries, preferred_element_type=jnp.float32)
        new_peak = jnp.maximum(row_peak, jnp.max(scores, axis=1))
        factor = jnp.exp(row_peak - new_peak)
        weights = jnp.exp(scores - new_peak[:, None, :])
        new_total = row_total * factor + jnp.sum(weights, axis=1)
        update = jnp.einsum(
            "khd,hkb->hdb",
            value_heads,
            weights.astype(jnp.bfloat16),
            preferred_element_type=jnp.float32,
        )
        return (new_peak, new_total, weighted * factor[:, None, :] + update)

    start_state = (
        jnp.full((HEADS, band_len), -1e30, jnp.float32),
        jnp.zeros((HEADS, band_len), jnp.float32),
        jnp.zeros((HEADS, HEAD_DIM, band_len), jnp.float32),
    )
    softmax_state = attend(start_state, slot_pairs)
    band_count = lax.axis_size("patch")

    def one_side(step_index, packed):
        state_now, ahead = packed
        ahead = banded_advance(ahead)
        return (attend(state_now, ahead), ahead)

    softmax_state, ahead = lax.fori_loop(0, band_count - 1, one_side, (softmax_state, slot_pairs))
    row_peak, row_total, weighted = banded_merged(softmax_state, ("chan", "sub"), banded_combine_parts)
    attended = (
        (weighted / row_total[:, None, :]).reshape(HEADS * HEAD_DIM, band_len).astype(jnp.bfloat16)
    )
    mixed = (
        projected.astype(jnp.float32) + jnp.dot(out_w, attended, preferred_element_type=jnp.float32)
    ).astype(jnp.bfloat16)
    columns = proj_out_w
    final_sum = resnet.astype(jnp.float32) + jnp.dot(
        columns,
        lax.all_gather(mixed, ("chan", "sub"), axis=0, tiled=True),
        preferred_element_type=jnp.float32,
    )
    return final_sum.astype(jnp.bfloat16)


def solution(mesh):
    in_specs = (
        P(("chan", "sub"), ("groups", "patch")),
        P("groups"),
        P(),
        P(("chan", "sub"), None),
        P(None, ("chan", "sub"), None),
        P(None, ("chan", "sub"), None),
        P(("chan", "sub"), None),
        P(("chan", "sub"), None),
        P(None, ("chan", "sub"), None),
        P(("chan", "sub"), None),
        P(("chan", "sub"), None),
    )
    out_specs = P(("chan", "sub"), ("groups", "patch"))

    def local(latent, *rest):
        few = mesh.shape["patch"] <= 4 and mesh.shape["chan"] == 2 and mesh.shape["sub"] == 2
        plan = whole_rows if few and latent.shape[1] == WIDTH else banded
        return plan(latent, *rest)

    return jax.shard_map(local, mesh=mesh, in_specs=in_specs, out_specs=out_specs, check_vma=False)
```

```python
import math

import jax
import jax.numpy as jnp
from jax import lax
from jax.experimental import pallas as pl
from jax.experimental.pallas import tpu as pltpu
from jax.sharding import PartitionSpec as P


C = 640
HEADS = 10
HEAD_DIM = 64
NGROUPS = 32
GROUP = C // NGROUPS
FREQ = 320
WIDTH = 256
BF16 = jnp.bfloat16
F32 = jnp.float32

OWN = C // 4
CHUNK = OWN // 2
FLIPS = (0, 2, 1, 3)


def own_place():
    return lax.axis_index("chan") * 2 + lax.axis_index("sub")


def call(kernel, outs, *args, scratch=(), flops=0, limit=24):
    specs = [pl.BlockSpec(memory_space=pltpu.VMEM)] * len(args)
    moved = sum(math.prod(a.shape) * a.dtype.itemsize for a in args)
    return pl.pallas_call(
        kernel,
        out_shape=[jax.ShapeDtypeStruct(s, t) for s, t in outs],
        in_specs=specs,
        out_specs=[pl.BlockSpec(memory_space=pltpu.VMEM)] * len(outs),
        scratch_shapes=[pltpu.VMEM(s, t) for s, t in scratch],
        compiler_params=pltpu.CompilerParams(vmem_limit_bytes=limit << 20),
        cost_estimate=pl.CostEstimate(flops=flops, transcendentals=0, bytes_accessed=moved),
    )(*args)


def group_sums(sums):
    wide = jnp.broadcast_to(sums, (sums.shape[0], 128))
    row = lax.broadcasted_iota(jnp.int32, wide.shape, 0)
    result = jnp.zeros_like(wide)
    for start in range(0, wide.shape[0], GROUP):
        inside = (row >= start) & (row < start + GROUP)
        total = jnp.sum(jnp.where(inside, wide, 0.0), axis=0, keepdims=True)
        result = jnp.where(inside, total, result)
    return result[:, :1]


def normal_form(rows, epsilon):
    cell_count = GROUP * len(rows) * rows[0].shape[1]
    centre = group_sums(sum(jnp.sum(row, axis=1, keepdims=True) for row in rows)) / cell_count
    shifted = [row - centre for row in rows]
    spread = group_sums(sum(jnp.sum(row * row, axis=1, keepdims=True) for row in shifted))
    scale = lax.rsqrt(spread / cell_count + epsilon)
    return [row * scale for row in shifted]


def silu(values):
    return values * jax.nn.sigmoid(values)


def first_norm(*refs):
    rows_ref, *chunk_refs = refs[-3:]
    pieces = refs[:-3]
    count = len(pieces) // 2
    position = lax.axis_index("patch")
    places = [position ^ by for by in range(count)]
    for piece, place in zip(pieces, places):
        rows_ref[place] = piece[...]
    for part, out in enumerate(chunk_refs):
        for side in range(2):
            values = [
                piece[part * CHUNK : (part + 1) * CHUNK, :].astype(F32)
                for piece in pieces[side * count : (side + 1) * count]
            ]
            for value, place in zip(normal_form(values, 1e-05), places):
                out[side, place] = silu(value).astype(BF16)


def arrange(weight, half_ref, *rest_refs):
    for tap in range(9):
        i, j = divmod(tap, 3)
        for part, rest_ref in enumerate(rest_refs):
            source = weight[tap, part * CHUNK : (part + 1) * CHUNK, :]
            for block in range(4):
                at = block * OWN
                to = (i * 4 + block) * CHUNK
                row = (part * 3 + j) * CHUNK
                half_ref[row : row + CHUNK, to : to + CHUNK] = source[:, at : at + CHUNK]
                row, at = j * CHUNK, at + CHUNK
                rest_ref[row : row + CHUNK, to : to + CHUNK] = source[:, at : at + CHUNK]


def place_blocks(blocks, padded):
    if len(blocks) == 2:
        blocks = [block.at[side] for block in blocks for side in range(2)]
    rows = blocks[0].shape[0]
    edge = jnp.zeros(padded.shape[1:], padded.dtype)
    padded[0] = edge
    padded[rows + 1] = edge
    for flip, block in zip(FLIPS, blocks):
        at = pl.multiple_of((own_place() ^ flip) * CHUNK, 16)
        padded[1 : rows + 1, pl.ds(at, CHUNK), :] = block[...]


def taps(weight, padded, row):
    window = padded[row : row + 3].reshape(3 * 4 * CHUNK, WIDTH)
    every = jnp.dot(weight[...], window, preferred_element_type=F32)
    lane = lax.broadcasted_iota(jnp.int32, (CHUNK, WIDTH), 1)
    results = []
    for start in range(0, every.shape[0], 3 * CHUNK):
        left, here, right = (
            every[start + j * CHUNK : start + (j + 1) * CHUNK] for j in range(3)
        )
        left = jnp.where(lane == 0, 0.0, pltpu.roll(left, 1, 1))
        right = jnp.where(lane == WIDTH - 1, 0.0, pltpu.roll(right, WIDTH - 1, 1))
        results.append(here + left + right)
    return results


def half_conv(*refs):
    *blocks, weight, one_ref, two_ref, padded = refs
    place_blocks(blocks, padded)
    for row in range(one_ref.shape[0]):
        one_ref[row], two_ref[row] = taps(weight, padded, row)


def first_conv(part):
    def kernel(*refs):
        *blocks, weight, half, bias, act_ref, padded = refs
        place_blocks(blocks, padded)
        added = bias[part * CHUNK : (part + 1) * CHUNK, :]
        rows = []
        for row in range(act_ref.shape[0]):
            (rest,) = taps(weight, padded, row)
            rows.append((half[row] + rest + added).astype(BF16).astype(F32))
        for row, value in enumerate(normal_form(rows, 1e-05)):
            act_ref[row] = silu(value).astype(BF16)

    return kernel


def second_conv(part):
    def kernel(*refs):
        *blocks, weight, half, latent, act_ref, resnet_ref, padded, sums = refs
        place_blocks(blocks, padded)
        rows = []
        for row in range(act_ref.shape[0]):
            (rest,) = taps(weight, padded, row)
            value = latent[row, part * CHUNK : (part + 1) * CHUNK, :].astype(F32) + (half[row] + rest)
            value = value.astype(BF16)
            sums[row] = value
            rows.append(value.astype(F32))
        resnet_ref[...] = sums[lax.axis_index("patch")]
        for row, value in enumerate(normal_form(rows, 1e-06)):
            act_ref[row] = value.astype(BF16)

    return kernel


def stack_rows(own, chan, sub, both, full):
    for flip, block in zip(FLIPS, (own, chan, sub, both)):
        full[pl.ds(pl.multiple_of((own_place() ^ flip) * OWN, 16), OWN), :] = block[...]


def stack_heads(q_own, kv_own, q_sub, kv_sub, q_ref, k_ref, v_ref):
    here = pl.multiple_of(lax.axis_index("sub") * OWN, 16)
    there = pl.multiple_of((1 - lax.axis_index("sub")) * OWN, 16)
    for at, q_part, kv_part in ((here, q_own, kv_own), (there, q_sub, kv_sub)):
        q_ref[pl.ds(at, OWN), :] = q_part[...]
        k_ref[pl.ds(at, OWN), :] = kv_part[0]
        v_ref[pl.ds(at, OWN), :] = kv_part[1]


def attend(*refs):
    blocks, refs = refs[:8], refs[8:]
    proj_w, q_w, k_w, v_w, out_ref, proj_ref, normed, projected, layered, keys, values = refs
    rows = normed.shape[0]
    for half in range(2):
        for flip, block in zip(FLIPS, blocks[half * 4 : half * 4 + 4]):
            at = pl.multiple_of((own_place() ^ flip) * OWN + half * CHUNK, 16)
            normed[:, pl.ds(at, CHUNK), :] = block[...]
    for row in range(rows):
        value = jnp.dot(proj_w[...], normed[row], preferred_element_type=F32).astype(BF16)
        projected[row] = value
        value = value.astype(F32)
        shifted = value - jnp.sum(value, axis=0, keepdims=True) / C
        spread = jnp.sum(shifted * shifted, axis=0, keepdims=True) / C
        layer = (shifted * lax.rsqrt(spread + 1e-05)).astype(BF16)
        layered[row] = layer
        at = slice(row * WIDTH, (row + 1) * WIDTH)
        keys[:, at] = jnp.dot(k_w[...], layer, preferred_element_type=F32).astype(BF16)
        values[:, at] = jnp.dot(v_w[...], layer, preferred_element_type=F32).astype(BF16)
    proj_ref[...] = projected[lax.axis_index("patch")]
    share = out_ref.shape[1]
    mine = layered[lax.axis_index("patch"), :, pl.ds(pl.multiple_of(lax.axis_index("sub") * share, 128), share)]
    query = (jnp.dot(q_w[...], mine, preferred_element_type=F32) * 0.125).astype(BF16)
    for head in range(query.shape[0] // HEAD_DIM):
        at = slice(head * HEAD_DIM, (head + 1) * HEAD_DIM)
        scores = lax.dot_general(
            keys[at, :], query[at], (((0,), (0,)), ((), ())), preferred_element_type=F32
        )
        weights = jnp.exp(scores - jnp.max(scores, axis=0, keepdims=True))
        total = jnp.sum(weights, axis=0, keepdims=True)
        weighted = jnp.dot(values[at, :], weights.astype(BF16), preferred_element_type=F32)
        out_ref[at, :] = (weighted / total).astype(BF16)


def finish(own, chan, sub, both, proj, res_one, res_two, out_w, last_w, out_ref, attended):
    channels, share = own.shape
    for flip, block in zip(FLIPS, (own, chan, sub, both)):
        place = own_place() ^ flip
        at = pl.multiple_of((place >> 1) * channels, 16)
        lanes = pl.multiple_of((place & 1) * share, 128)
        attended[pl.ds(at, channels), pl.ds(lanes, share)] = block[...]
    mixed = proj[...].astype(F32) + jnp.dot(
        out_w[...], attended[...], preferred_element_type=F32
    )
    last = jnp.dot(last_w[...], mixed.astype(BF16), preferred_element_type=F32)
    for part, res in enumerate((res_one, res_two)):
        at = slice(part * CHUNK, (part + 1) * CHUNK)
        out_ref[at, :] = (res[...].astype(F32) + last[at]).astype(BF16)


def swapped(array, axis, by=1):
    return lax.ppermute(array, axis, [(i, i ^ by) for i in range(lax.axis_size(axis))])


def embedding_of(timestep):
    half_width = FREQ // 2
    frequency = jnp.exp(-math.log(10000.0) * jnp.arange(half_width, dtype=F32) / half_width)
    angles = timestep[0].astype(F32) * frequency
    return jnp.concatenate([jnp.cos(angles), jnp.sin(angles)]).astype(BF16)


def time_bias(embedded, time_w1, time_proj, bias_ref):
    contract_last = (((1,), (1,)), ((), ()))
    wide = jnp.broadcast_to(embedded[...], (16, FREQ))
    hidden = silu(jnp.dot(wide, time_w1[...], preferred_element_type=F32))
    act = silu(hidden).astype(BF16)
    bias_ref[...] = lax.dot_general(
        time_proj[...], act, contract_last, preferred_element_type=F32
    )[:, :1]


def whole_rows(
    latent, timestep, time_w1, time_proj, conv1_w, conv2_w, proj_in_w, q_w, kv_w, out_w, proj_out_w
):
    rows = lax.axis_size("patch")
    chunk = (rows, CHUNK, WIDTH)
    padded = ((rows + 2, 4 * CHUNK, WIDTH), BF16)
    tap_flops = 2 * 3 * CHUNK * 12 * CHUNK * rows * WIDTH
    barrier = lax.optimization_barrier

    def arranged(weight):
        outs = [((width * CHUNK, 12 * CHUNK), BF16) for width in (6, 3, 3)]
        return call(arrange, outs, weight, flops=10**9)

    def stacked(blocks):
        return call(stack_rows, [((C, C), BF16)], *blocks, flops=10**8)[0]

    def exchanged(own, *beside):
        chan = swapped(own, "chan")
        own, chan, beside = barrier((own, chan, beside))
        sub = swapped(own, "sub")
        return (own, chan, sub, swapped(chan, "sub")), beside

    pieces = [latent] + [swapped(latent, "patch", by) for by in range(1, rows)]
    others = [swapped(piece, "chan") for piece in pieces]
    proj_in_chan = swapped(proj_in_w, "chan")
    embedded = embedding_of(timestep)[None]
    (_, *heads_w), embedded = barrier(((pieces[-1], q_w, kv_w), embedded))
    (bias,) = call(time_bias, [((OWN, 1), F32)], embedded, time_w1.T, time_proj, flops=10**8)
    heads_w = (*heads_w, *(swapped(weight, "sub") for weight in heads_w))
    others, conv1_w, bias = barrier((others, arranged(conv1_w), bias))
    pair = (2,) + chunk
    latent_rows, one, two = call(
        first_norm, [((rows, OWN, WIDTH), BF16), (pair, BF16), (pair, BF16)], *pieces, *others,
    )
    one, two = (one, swapped(one, "sub")), (two, swapped(two, "sub"))

    def halves(blocks, weight):
        return call(
            half_conv, [(chunk, F32)] * 2, *blocks, weight, scratch=[padded],
            flops=2 * tap_flops,
        )

    half = halves(one, conv1_w[0])
    one, two = (
        call(
            first_conv(part), [(chunk, BF16)], *two, conv1_w[1 + part], half[part], bias,
            scratch=[padded], flops=tap_flops,
        )[0]
        for part in range(2)
    )
    _, heads_w, conv2_w, proj_in_chan = barrier((one, heads_w, conv2_w, proj_in_chan))
    heads_w = call(stack_heads, [((2 * OWN, C), BF16)] * 3, *heads_w, flops=10**8)
    proj_in = (
        proj_in_w, proj_in_chan, swapped(proj_in_w, "sub"),
        swapped(proj_in_chan, "sub"),
    )
    one, (heads_w, conv2_w, proj_in) = exchanged(one, heads_w, arranged(conv2_w), proj_in)
    two, _ = exchanged(two)
    half = halves(one, conv2_w[0])
    (one, res_one), (two, res_two) = (
        call(
            second_conv(part), [(chunk, BF16), ((CHUNK, WIDTH), BF16)],
            *two, conv2_w[1 + part], half[part], latent_rows,
            scratch=[padded, (chunk, BF16)], flops=tap_flops,
        )
        for part in range(2)
    )
    _, proj_in, out_w = barrier((one, proj_in, out_w))
    one, (proj_in, out_sub) = exchanged(one, stacked(proj_in), swapped(out_w, "sub"))
    two, _ = exchanged(two)
    _, out_chan = barrier((two, out_w))
    out_chan = swapped(out_chan, "chan")
    share = WIDTH // 2
    attended, projected = call(
        attend, [((2 * OWN, share), BF16), ((C, WIDTH), BF16)],
        *one, *two, proj_in, *heads_w,
        scratch=[((rows, C, WIDTH), BF16)] * 3 + [((2 * OWN, rows * WIDTH), BF16)] * 2,
        flops=4 * 10**9, limit=32,
    )
    _, out_chan = barrier((attended, out_chan))
    out_all = stacked((out_w, out_chan, out_sub, swapped(out_chan, "sub")))
    attended, (out_all,) = exchanged(attended, out_all)
    return call(
        finish, [((OWN, WIDTH), BF16)], *attended, projected, res_one, res_two,
        out_all, proj_out_w, scratch=[((C, WIDTH), BF16)],
    )[0]


def banded_with_halo(cells, sides, width):
    for axis, dim in sides:
        count = lax.axis_size(axis)
        ends = count - 1
        head = lax.slice_in_dim(cells, 0, width, axis=dim)
        tail = lax.slice_in_dim(cells, cells.shape[dim] - width, cells.shape[dim], axis=dim)
        cells = jnp.concatenate(
            [
                lax.ppermute(tail, axis, [(i, (i + 1) % count) for i in range(ends)]),
                cells,
                lax.ppermute(head, axis, [((i + 1) % count, i) for i in range(ends)]),
            ],
            axis=dim,
        )
    return cells


def banded_from_behind(array, axis, by):
    count = lax.axis_size(axis)
    return lax.ppermute(array, axis, [(i, (i + by) % count) for i in range(count)])


def banded_merged(array, axis, combine):
    everything = jax.tree.map(lambda part: lax.all_gather(part, axis), array)
    first = jax.tree.map(lambda part: part[0], everything)

    def turn(k, so_far):
        return combine(so_far, jax.tree.map(lambda part: part[k], everything))

    return lax.fori_loop(1, lax.axis_size(axis), turn, first)


def banded_group_norm(values, epsilon):
    channels, band_len = values.shape
    group_size = C // NGROUPS
    grouped = values.reshape(channels // group_size, group_size, band_len)
    cell_count = group_size * band_len * lax.axis_size("patch")
    centre = lax.psum(jnp.sum(grouped, axis=(1, 2)), "patch") / cell_count
    shifted = grouped - centre[:, None, None]
    spread = lax.psum(jnp.sum(shifted * shifted, axis=(1, 2)), "patch") / cell_count
    normal_form = (grouped - centre[:, None, None]) * lax.rsqrt(spread + epsilon)[:, None, None]
    return normal_form.reshape(channels, band_len)


def banded_convolve(active, weight):
    _, band_len = active.shape
    height = band_len // WIDTH
    whole_rows = lax.all_gather(active, ("chan", "sub"), axis=0, tiled=True)
    image_grid = whole_rows.reshape(whole_rows.shape[0], height, WIDTH)
    padded = banded_with_halo(image_grid, (("patch", 1),), 1)
    channels = padded.shape[0]
    padded = jnp.pad(padded, ((0, 0), (0, 0), (1, 1)))
    running = jnp.zeros((weight.shape[1], band_len), jnp.float32)
    for offset in range(9):
        row_step, col_step = divmod(offset, 3)
        window = padded[:, row_step : row_step + height, col_step : col_step + WIDTH].reshape(
            channels, band_len
        )
        running = running + jnp.dot(weight[offset], window, preferred_element_type=jnp.float32)
    return running


def banded_combine_parts(earlier_part, later_part):
    peak_one, total_one, sums_one = earlier_part
    peak_two, total_two, sums_two = later_part
    new_peak = jnp.maximum(peak_one, peak_two)
    factor_one = jnp.exp(peak_one - new_peak)
    factor_two = jnp.exp(peak_two - new_peak)
    new_total = total_one * factor_one + total_two * factor_two
    new_sums = sums_one * factor_one[:, None, :] + sums_two * factor_two[:, None, :]
    return (new_peak, new_total, new_sums)


def banded_advance(kv_piece):
    return banded_from_behind(kv_piece, "patch", 1)


def banded(
    latent, timestep, time_w1, time_proj, conv1_w, conv2_w, proj_in_w, q_w, kv_w, out_w, proj_out_w
):
    latent_f32 = latent.astype(jnp.float32)
    band_len = latent.shape[1]
    half_width = FREQ // 2
    frequency = jnp.exp(-math.log(10000.0) * jnp.arange(half_width, dtype=jnp.float32) / half_width)
    angles = timestep[0].astype(jnp.float32) * frequency
    embedded = jnp.concatenate([jnp.cos(angles), jnp.sin(angles)]).astype(jnp.bfloat16)
    time_hidden = jax.nn.silu(jnp.dot(time_w1, embedded, preferred_element_type=jnp.float32))
    time_bias = jnp.dot(
        time_proj, jax.nn.silu(time_hidden).astype(jnp.bfloat16), preferred_element_type=jnp.float32
    )
    act_one = jax.nn.silu(banded_group_norm(latent_f32, 1e-05)).astype(jnp.bfloat16)
    conv_one = (banded_convolve(act_one, conv1_w) + time_bias[:, None]).astype(jnp.bfloat16)
    act_two = jax.nn.silu(banded_group_norm(conv_one.astype(jnp.float32), 1e-05)).astype(jnp.bfloat16)
    resnet = (latent_f32 + banded_convolve(act_two, conv2_w)).astype(jnp.bfloat16)
    normed = banded_group_norm(resnet.astype(jnp.float32), 1e-06).astype(jnp.bfloat16)
    columns = proj_in_w
    projected = jnp.dot(
        columns,
        lax.all_gather(normed, ("chan", "sub"), axis=0, tiled=True),
        preferred_element_type=jnp.float32,
    ).astype(jnp.bfloat16)
    whole_proj = lax.all_gather(projected, ("chan", "sub"), axis=0, tiled=True).astype(jnp.float32)
    centre = jnp.mean(whole_proj, axis=0, keepdims=True)
    spread = jnp.mean((whole_proj - centre) * (whole_proj - centre), axis=0, keepdims=True)
    layer_normed = ((whole_proj - centre) / jnp.sqrt(spread + 1e-05)).astype(jnp.bfloat16)
    query_own = (jnp.dot(q_w, layer_normed, preferred_element_type=jnp.float32) * 0.125).astype(
        jnp.bfloat16
    )
    queries = lax.all_gather(query_own, ("chan", "sub"), axis=0, tiled=True).reshape(
        HEADS, HEAD_DIM, band_len
    )
    key_value = jnp.einsum(
        "joc,cb->jbo", kv_w, layer_normed, preferred_element_type=jnp.float32
    ).astype(jnp.bfloat16)
    slot_pairs = lax.all_to_all(key_value, ("chan", "sub"), split_axis=1, concat_axis=2, tiled=True)

    def attend(softmax_state, kv_piece):
        row_peak, row_total, weighted = softmax_state
        slot_len = kv_piece.shape[1]
        key_heads = kv_piece[0].reshape(slot_len, HEADS, HEAD_DIM)
        value_heads = kv_piece[1].reshape(slot_len, HEADS, HEAD_DIM)
        scores = jnp.einsum("khd,hdb->hkb", key_heads, queries, preferred_element_type=jnp.float32)
        new_peak = jnp.maximum(row_peak, jnp.max(scores, axis=1))
        factor = jnp.exp(row_peak - new_peak)
        weights = jnp.exp(scores - new_peak[:, None, :])
        new_total = row_total * factor + jnp.sum(weights, axis=1)
        update = jnp.einsum(
            "khd,hkb->hdb",
            value_heads,
            weights.astype(jnp.bfloat16),
            preferred_element_type=jnp.float32,
        )
        return (new_peak, new_total, weighted * factor[:, None, :] + update)

    start_state = (
        jnp.full((HEADS, band_len), -1e30, jnp.float32),
        jnp.zeros((HEADS, band_len), jnp.float32),
        jnp.zeros((HEADS, HEAD_DIM, band_len), jnp.float32),
    )
    softmax_state = attend(start_state, slot_pairs)
    band_count = lax.axis_size("patch")

    def one_side(step_index, packed):
        state_now, ahead = packed
        ahead = banded_advance(ahead)
        return (attend(state_now, ahead), ahead)

    softmax_state, _ = lax.fori_loop(0, band_count - 1, one_side, (softmax_state, slot_pairs))
    _, row_total, weighted = banded_merged(softmax_state, ("chan", "sub"), banded_combine_parts)
    attended = (
        (weighted / row_total[:, None, :]).reshape(HEADS * HEAD_DIM, band_len).astype(jnp.bfloat16)
    )
    mixed = (
        projected.astype(jnp.float32) + jnp.dot(out_w, attended, preferred_element_type=jnp.float32)
    ).astype(jnp.bfloat16)
    columns = proj_out_w
    final_sum = resnet.astype(jnp.float32) + jnp.dot(
        columns,
        lax.all_gather(mixed, ("chan", "sub"), axis=0, tiled=True),
        preferred_element_type=jnp.float32,
    )
    return final_sum.astype(jnp.bfloat16)


def solution(mesh):
    in_specs = (
        P(("chan", "sub"), ("groups", "patch")),
        P("groups"),
        P(),
        P(("chan", "sub"), None),
        P(None, ("chan", "sub"), None),
        P(None, ("chan", "sub"), None),
        P(("chan", "sub"), None),
        P(("chan", "sub"), None),
        P(None, ("chan", "sub"), None),
        P(("chan", "sub"), None),
        P(("chan", "sub"), None),
    )
    out_specs = P(("chan", "sub"), ("groups", "patch"))

    few = mesh.shape["patch"] in (1, 2, 4) and mesh.shape["chan"] == 2 and mesh.shape["sub"] == 2

    def local(latent, *rest):
        if not few or latent.shape[1] != WIDTH:
            return banded(latent, *rest)
        return whole_rows(latent, *rest)

    return jax.shard_map(local, mesh=mesh, in_specs=in_specs, out_specs=out_specs, check_vma=False)
```

```python
import math

import jax
import jax.numpy as jnp
from jax import lax
from jax.experimental import pallas as pl
from jax.experimental.pallas import tpu as pltpu
from jax.sharding import PartitionSpec as P


C = 640
HEADS = 10
HEAD_DIM = 64
NGROUPS = 32
GROUP = C // NGROUPS
FREQ = 320
WIDTH = 256
BF16 = jnp.bfloat16
F32 = jnp.float32

OWN = C // 4
CHUNK = OWN // 2
FLIPS = (0, 2, 1, 3)


def own_place():
    return lax.axis_index("chan") * 2 + lax.axis_index("sub")


def call(kernel, outs, *args, scratch=(), flops=0, limit=24):
    specs = [pl.BlockSpec(memory_space=pltpu.VMEM)] * len(args)
    moved = sum(math.prod(a.shape) * a.dtype.itemsize for a in args)
    return pl.pallas_call(
        kernel,
        out_shape=[jax.ShapeDtypeStruct(s, t) for s, t in outs],
        in_specs=specs,
        out_specs=[pl.BlockSpec(memory_space=pltpu.VMEM)] * len(outs),
        scratch_shapes=[pltpu.VMEM(s, t) for s, t in scratch],
        compiler_params=pltpu.CompilerParams(vmem_limit_bytes=limit << 20),
        cost_estimate=pl.CostEstimate(flops=flops, transcendentals=0, bytes_accessed=moved),
    )(*args)


def group_sums(sums):
    wide = jnp.broadcast_to(sums, (sums.shape[0], 128))
    row = lax.broadcasted_iota(jnp.int32, wide.shape, 0)
    result = jnp.zeros_like(wide)
    for start in range(0, wide.shape[0], GROUP):
        inside = (row >= start) & (row < start + GROUP)
        total = jnp.sum(jnp.where(inside, wide, 0.0), axis=0, keepdims=True)
        result = jnp.where(inside, total, result)
    return result[:, :1]


def normal_form(rows, epsilon):
    cell_count = GROUP * len(rows) * rows[0].shape[1]
    centre = group_sums(sum(jnp.sum(row, axis=1, keepdims=True) for row in rows)) / cell_count
    shifted = [row - centre for row in rows]
    spread = group_sums(sum(jnp.sum(row * row, axis=1, keepdims=True) for row in shifted))
    scale = lax.rsqrt(spread / cell_count + epsilon)
    return [row * scale for row in shifted]


def silu(values):
    return values * jax.nn.sigmoid(values)


def first_norm(*refs):
    rows_ref, *chunk_refs = refs[-3:]
    pieces = refs[:-3]
    count = len(pieces) // 2
    position = lax.axis_index("patch")
    places = [position ^ by for by in range(count)]
    for piece, place in zip(pieces, places):
        rows_ref[place] = piece[...]
    for part, out in enumerate(chunk_refs):
        for side in range(2):
            values = [
                piece[part * CHUNK : (part + 1) * CHUNK, :].astype(F32)
                for piece in pieces[side * count : (side + 1) * count]
            ]
            for value, place in zip(normal_form(values, 1e-05), places):
                out[side, place] = silu(value).astype(BF16)


def arrange(weight, half_ref, *rest_refs):
    for tap in range(9):
        i, j = divmod(tap, 3)
        for part, rest_ref in enumerate(rest_refs):
            source = weight[tap, part * CHUNK : (part + 1) * CHUNK, :]
            for block in range(4):
                at = block * OWN
                to = (i * 4 + block) * CHUNK
                row = (part * 3 + j) * CHUNK
                half_ref[row : row + CHUNK, to : to + CHUNK] = source[:, at : at + CHUNK]
                row, at = j * CHUNK, at + CHUNK
                rest_ref[row : row + CHUNK, to : to + CHUNK] = source[:, at : at + CHUNK]


def place_blocks(blocks, padded):
    if len(blocks) == 2:
        blocks = [block.at[side] for block in blocks for side in range(2)]
    rows = blocks[0].shape[0]
    edge = jnp.zeros(padded.shape[1:], padded.dtype)
    padded[0] = edge
    padded[rows + 1] = edge
    for flip, block in zip(FLIPS, blocks):
        at = pl.multiple_of((own_place() ^ flip) * CHUNK, 16)
        padded[1 : rows + 1, pl.ds(at, CHUNK), :] = block[...]


def taps(weight, padded, row):
    window = padded[row : row + 3].reshape(3 * 4 * CHUNK, WIDTH)
    every = jnp.dot(weight[...], window, preferred_element_type=F32)
    lane = lax.broadcasted_iota(jnp.int32, (CHUNK, WIDTH), 1)
    results = []
    for start in range(0, every.shape[0], 3 * CHUNK):
        left, here, right = (
            every[start + j * CHUNK : start + (j + 1) * CHUNK] for j in range(3)
        )
        left = jnp.where(lane == 0, 0.0, pltpu.roll(left, 1, 1))
        right = jnp.where(lane == WIDTH - 1, 0.0, pltpu.roll(right, WIDTH - 1, 1))
        results.append(here + left + right)
    return results


def half_conv(*refs):
    *blocks, weight, one_ref, two_ref, padded = refs
    place_blocks(blocks, padded)
    for row in range(one_ref.shape[0]):
        one_ref[row], two_ref[row] = taps(weight, padded, row)


def first_conv(part):
    def kernel(*refs):
        *blocks, weight, half, bias, act_ref, padded = refs
        place_blocks(blocks, padded)
        added = bias[part * CHUNK : (part + 1) * CHUNK, :]
        rows = []
        for row in range(act_ref.shape[0]):
            (rest,) = taps(weight, padded, row)
            rows.append((half[row] + rest + added).astype(BF16).astype(F32))
        for row, value in enumerate(normal_form(rows, 1e-05)):
            act_ref[row] = silu(value).astype(BF16)

    return kernel


def second_conv(part):
    def kernel(*refs):
        *blocks, weight, half, latent, act_ref, resnet_ref, padded, sums = refs
        place_blocks(blocks, padded)
        rows = []
        for row in range(act_ref.shape[0]):
            (rest,) = taps(weight, padded, row)
            value = latent[row, part * CHUNK : (part + 1) * CHUNK, :].astype(F32) + (half[row] + rest)
            value = value.astype(BF16)
            sums[row] = value
            rows.append(value.astype(F32))
        resnet_ref[...] = sums[lax.axis_index("patch")]
        for row, value in enumerate(normal_form(rows, 1e-06)):
            act_ref[row] = value.astype(BF16)

    return kernel


def stack_rows(own, chan, sub, both, full):
    for flip, block in zip(FLIPS, (own, chan, sub, both)):
        full[pl.ds(pl.multiple_of((own_place() ^ flip) * OWN, 16), OWN), :] = block[...]


def stack_heads(q_own, kv_own, q_sub, kv_sub, q_ref, kv_ref):
    here = lax.axis_index("sub") * OWN
    for at, q_part, kv_part in ((here, q_own, kv_own), (OWN - here, q_sub, kv_sub)):
        at = pl.multiple_of(at, 16)
        q_ref[pl.ds(at, OWN), :] = q_part[...]
        kv_ref[pl.ds(at, OWN), :] = kv_part[0]
        kv_ref[pl.ds(at + 2 * OWN, OWN), :] = kv_part[1]


def attend(*refs):
    blocks, refs = refs[:8], refs[8:]
    proj_w, q_w, kv_w, out_ref, proj_ref, normed, projected, layered, heads = refs
    rows = normed.shape[0]
    for half in range(2):
        for flip, block in zip(FLIPS, blocks[half * 4 : half * 4 + 4]):
            at = pl.multiple_of((own_place() ^ flip) * OWN + half * CHUNK, 16)
            normed[:, pl.ds(at, CHUNK), :] = block[...]
    for row in range(rows):
        value = jnp.dot(proj_w[...], normed[row], preferred_element_type=F32).astype(BF16)
        projected[row] = value
        value = value.astype(F32)
        shifted = value - jnp.sum(value, axis=0, keepdims=True) / C
        spread = jnp.sum(shifted * shifted, axis=0, keepdims=True) / C
        layer = (shifted * lax.rsqrt(spread + 1e-05)).astype(BF16)
        layered[row] = layer
        at = slice(row * WIDTH, (row + 1) * WIDTH)
        heads[:, at] = jnp.dot(kv_w[...], layer, preferred_element_type=F32).astype(BF16)
    proj_ref[...] = projected[lax.axis_index("patch")]
    share = out_ref.shape[1]
    mine = layered[lax.axis_index("patch"), :, pl.ds(pl.multiple_of(lax.axis_index("sub") * share, 128), share)]
    query = (jnp.dot(q_w[...], mine, preferred_element_type=F32) * 0.125).astype(BF16)
    channels = query.shape[0]
    for start in range(0, channels, HEAD_DIM):
        at = slice(start, start + HEAD_DIM)
        scores = lax.dot_general(
            heads[at, :], query[at], (((0,), (0,)), ((), ())), preferred_element_type=F32
        )
        weights = jnp.exp(scores - jnp.max(scores, axis=0, keepdims=True))
        total = jnp.sum(weights, axis=0, keepdims=True)
        weighted = jnp.dot(
            heads[channels + start : channels + start + HEAD_DIM, :],
            weights.astype(BF16),
            preferred_element_type=F32,
        )
        out_ref[at, :] = (weighted / total).astype(BF16)


def finish(own, chan, sub, both, proj, res_one, res_two, out_w, last_w, out_ref, attended):
    channels, share = own.shape
    for flip, block in zip(FLIPS, (own, chan, sub, both)):
        place = own_place() ^ flip
        at = pl.multiple_of((place >> 1) * channels, 16)
        lanes = pl.multiple_of((place & 1) * share, 128)
        attended[pl.ds(at, channels), pl.ds(lanes, share)] = block[...]
    mixed = proj[...].astype(F32) + jnp.dot(
        out_w[...], attended[...], preferred_element_type=F32
    )
    last = jnp.dot(last_w[...], mixed.astype(BF16), preferred_element_type=F32)
    for part, res in enumerate((res_one, res_two)):
        at = slice(part * CHUNK, (part + 1) * CHUNK)
        out_ref[at, :] = (res[...].astype(F32) + last[at]).astype(BF16)


def swapped(array, axis, by=1):
    return lax.ppermute(array, axis, [(i, i ^ by) for i in range(lax.axis_size(axis))])


def embedding_of(timestep):
    half_width = FREQ // 2
    frequency = jnp.exp(-math.log(10000.0) * jnp.arange(half_width, dtype=F32) / half_width)
    angles = timestep[0].astype(F32) * frequency
    return jnp.concatenate([jnp.cos(angles), jnp.sin(angles)]).astype(BF16)


def time_bias(embedded, time_w1, time_proj, bias_ref):
    contract_last = (((1,), (1,)), ((), ()))
    wide = jnp.broadcast_to(embedded[...], (16, FREQ))
    hidden = silu(jnp.dot(wide, time_w1[...], preferred_element_type=F32))
    act = silu(hidden).astype(BF16)
    bias_ref[...] = lax.dot_general(
        time_proj[...], act, contract_last, preferred_element_type=F32
    )[:, :1]


def whole_rows(
    latent, timestep, time_w1, time_proj, conv1_w, conv2_w, proj_in_w, q_w, kv_w, out_w, proj_out_w
):
    rows = lax.axis_size("patch")
    chunk = (rows, CHUNK, WIDTH)
    padded = ((rows + 2, 4 * CHUNK, WIDTH), BF16)
    tap_flops = 2 * 3 * CHUNK * 12 * CHUNK * rows * WIDTH
    barrier = lax.optimization_barrier

    def arranged(weight):
        outs = [((width * CHUNK, 12 * CHUNK), BF16) for width in (6, 3, 3)]
        return call(arrange, outs, weight, flops=10**9)

    def stacked(blocks):
        return call(stack_rows, [((C, C), BF16)], *blocks, flops=10**8)[0]

    def exchanged(own, *beside):
        chan = swapped(own, "chan")
        own, chan, beside = barrier((own, chan, beside))
        sub = swapped(own, "sub")
        return (own, chan, sub, swapped(chan, "sub")), beside

    pieces = [latent] + [swapped(latent, "patch", by) for by in range(1, rows)]
    others = [swapped(piece, "chan") for piece in pieces]
    proj_in_chan = swapped(proj_in_w, "chan")
    _, timestep, *heads_w = barrier((pieces[-1], timestep, q_w, kv_w))
    embedded = embedding_of(timestep)[None]
    heads_w = (*heads_w, *(swapped(weight, "sub") for weight in heads_w))
    others, conv1_w, embedded = barrier((others, arranged(conv1_w), embedded))
    pair = (2,) + chunk
    latent_rows, one, two = call(
        first_norm, [((rows, OWN, WIDTH), BF16), (pair, BF16), (pair, BF16)], *pieces, *others,
    )
    one, two = (one, swapped(one, "sub")), (two, swapped(two, "sub"))
    (bias,) = call(time_bias, [((OWN, 1), F32)], embedded, time_w1.T, time_proj, flops=10**8)

    def halves(blocks, weight):
        return call(
            half_conv, [(chunk, F32)] * 2, *blocks, weight, scratch=[padded],
            flops=2 * tap_flops,
        )

    half = halves(one, conv1_w[0])
    one, two = (
        call(
            first_conv(part), [(chunk, BF16)], *two, conv1_w[1 + part], half[part], bias,
            scratch=[padded], flops=tap_flops,
        )[0]
        for part in range(2)
    )
    _, heads_w, conv2_w = barrier((one, heads_w, conv2_w))
    heads_w = call(
        stack_heads, [((2 * OWN, C), BF16), ((4 * OWN, C), BF16)], *heads_w,
        flops=10**8,
    )
    proj_in_sub = swapped(proj_in_w, "sub")
    one, (heads_w, conv2_w, proj_in_sub) = exchanged(one, heads_w, arranged(conv2_w), proj_in_sub)
    two, _ = exchanged(two)
    half = halves(one, conv2_w[0])
    (one, res_one), (two, res_two) = (
        call(
            second_conv(part), [(chunk, BF16), ((CHUNK, WIDTH), BF16)],
            *two, conv2_w[1 + part], half[part], latent_rows,
            scratch=[padded, (chunk, BF16)], flops=tap_flops,
        )
        for part in range(2)
    )
    _, proj_in_chan, out_w = barrier((one, proj_in_chan, out_w))
    proj_in = (proj_in_w, proj_in_chan, proj_in_sub, swapped(proj_in_chan, "sub"))
    one, (proj_in, out_sub) = exchanged(one, stacked(proj_in), swapped(out_w, "sub"))
    two, _ = exchanged(two)
    out_chan = swapped(out_w, "chan")
    share = WIDTH // 2
    attended, projected = call(
        attend, [((2 * OWN, share), BF16), ((C, WIDTH), BF16)],
        *one, *two, proj_in, *heads_w,
        scratch=[((rows, C, WIDTH), BF16)] * 3 + [((4 * OWN, rows * WIDTH), BF16)],
        flops=4 * 10**9, limit=32,
    )
    _, out_chan = barrier((attended, out_chan))
    out_all = stacked((out_w, out_chan, out_sub, swapped(out_chan, "sub")))
    attended, (out_all,) = exchanged(attended, out_all)
    return call(
        finish, [((OWN, WIDTH), BF16)], *attended, projected, res_one, res_two,
        out_all, proj_out_w, scratch=[((C, WIDTH), BF16)],
    )[0]


def banded_with_halo(cells, sides, width):
    for axis, dim in sides:
        count = lax.axis_size(axis)
        ends = count - 1
        head = lax.slice_in_dim(cells, 0, width, axis=dim)
        tail = lax.slice_in_dim(cells, cells.shape[dim] - width, cells.shape[dim], axis=dim)
        cells = jnp.concatenate(
            [
                lax.ppermute(tail, axis, [(i, (i + 1) % count) for i in range(ends)]),
                cells,
                lax.ppermute(head, axis, [((i + 1) % count, i) for i in range(ends)]),
            ],
            axis=dim,
        )
    return cells


def banded_from_behind(array, axis, by):
    count = lax.axis_size(axis)
    return lax.ppermute(array, axis, [(i, (i + by) % count) for i in range(count)])


def banded_merged(array, axis, combine):
    everything = jax.tree.map(lambda part: lax.all_gather(part, axis), array)
    first = jax.tree.map(lambda part: part[0], everything)

    def turn(k, so_far):
        return combine(so_far, jax.tree.map(lambda part: part[k], everything))

    return lax.fori_loop(1, lax.axis_size(axis), turn, first)


def banded_group_norm(values, epsilon):
    channels, band_len = values.shape
    group_size = C // NGROUPS
    grouped = values.reshape(channels // group_size, group_size, band_len)
    cell_count = group_size * band_len * lax.axis_size("patch")
    centre = lax.psum(jnp.sum(grouped, axis=(1, 2)), "patch") / cell_count
    shifted = grouped - centre[:, None, None]
    spread = lax.psum(jnp.sum(shifted * shifted, axis=(1, 2)), "patch") / cell_count
    normal_form = (grouped - centre[:, None, None]) * lax.rsqrt(spread + epsilon)[:, None, None]
    return normal_form.reshape(channels, band_len)


def banded_convolve(active, weight):
    _, band_len = active.shape
    height = band_len // WIDTH
    whole_rows = lax.all_gather(active, ("chan", "sub"), axis=0, tiled=True)
    image_grid = whole_rows.reshape(whole_rows.shape[0], height, WIDTH)
    padded = banded_with_halo(image_grid, (("patch", 1),), 1)
    channels = padded.shape[0]
    padded = jnp.pad(padded, ((0, 0), (0, 0), (1, 1)))
    running = jnp.zeros((weight.shape[1], band_len), jnp.float32)
    for offset in range(9):
        row_step, col_step = divmod(offset, 3)
        window = padded[:, row_step : row_step + height, col_step : col_step + WIDTH].reshape(
            channels, band_len
        )
        running = running + jnp.dot(weight[offset], window, preferred_element_type=jnp.float32)
    return running


def banded_combine_parts(earlier_part, later_part):
    peak_one, total_one, sums_one = earlier_part
    peak_two, total_two, sums_two = later_part
    new_peak = jnp.maximum(peak_one, peak_two)
    factor_one = jnp.exp(peak_one - new_peak)
    factor_two = jnp.exp(peak_two - new_peak)
    new_total = total_one * factor_one + total_two * factor_two
    new_sums = sums_one * factor_one[:, None, :] + sums_two * factor_two[:, None, :]
    return (new_peak, new_total, new_sums)


def banded_advance(kv_piece):
    return banded_from_behind(kv_piece, "patch", 1)


def banded(
    latent, timestep, time_w1, time_proj, conv1_w, conv2_w, proj_in_w, q_w, kv_w, out_w, proj_out_w
):
    latent_f32 = latent.astype(jnp.float32)
    band_len = latent.shape[1]
    half_width = FREQ // 2
    frequency = jnp.exp(-math.log(10000.0) * jnp.arange(half_width, dtype=jnp.float32) / half_width)
    angles = timestep[0].astype(jnp.float32) * frequency
    embedded = jnp.concatenate([jnp.cos(angles), jnp.sin(angles)]).astype(jnp.bfloat16)
    time_hidden = jax.nn.silu(jnp.dot(time_w1, embedded, preferred_element_type=jnp.float32))
    time_bias = jnp.dot(
        time_proj, jax.nn.silu(time_hidden).astype(jnp.bfloat16), preferred_element_type=jnp.float32
    )
    act_one = jax.nn.silu(banded_group_norm(latent_f32, 1e-05)).astype(jnp.bfloat16)
    conv_one = (banded_convolve(act_one, conv1_w) + time_bias[:, None]).astype(jnp.bfloat16)
    act_two = jax.nn.silu(banded_group_norm(conv_one.astype(jnp.float32), 1e-05)).astype(jnp.bfloat16)
    resnet = (latent_f32 + banded_convolve(act_two, conv2_w)).astype(jnp.bfloat16)
    normed = banded_group_norm(resnet.astype(jnp.float32), 1e-06).astype(jnp.bfloat16)
    columns = proj_in_w
    projected = jnp.dot(
        columns,
        lax.all_gather(normed, ("chan", "sub"), axis=0, tiled=True),
        preferred_element_type=jnp.float32,
    ).astype(jnp.bfloat16)
    whole_proj = lax.all_gather(projected, ("chan", "sub"), axis=0, tiled=True).astype(jnp.float32)
    centre = jnp.mean(whole_proj, axis=0, keepdims=True)
    spread = jnp.mean((whole_proj - centre) * (whole_proj - centre), axis=0, keepdims=True)
    layer_normed = ((whole_proj - centre) / jnp.sqrt(spread + 1e-05)).astype(jnp.bfloat16)
    query_own = (jnp.dot(q_w, layer_normed, preferred_element_type=jnp.float32) * 0.125).astype(
        jnp.bfloat16
    )
    queries = lax.all_gather(query_own, ("chan", "sub"), axis=0, tiled=True).reshape(
        HEADS, HEAD_DIM, band_len
    )
    key_value = jnp.einsum(
        "joc,cb->jbo", kv_w, layer_normed, preferred_element_type=jnp.float32
    ).astype(jnp.bfloat16)
    slot_pairs = lax.all_to_all(key_value, ("chan", "sub"), split_axis=1, concat_axis=2, tiled=True)

    def attend(softmax_state, kv_piece):
        row_peak, row_total, weighted = softmax_state
        slot_len = kv_piece.shape[1]
        key_heads = kv_piece[0].reshape(slot_len, HEADS, HEAD_DIM)
        value_heads = kv_piece[1].reshape(slot_len, HEADS, HEAD_DIM)
        scores = jnp.einsum("khd,hdb->hkb", key_heads, queries, preferred_element_type=jnp.float32)
        new_peak = jnp.maximum(row_peak, jnp.max(scores, axis=1))
        factor = jnp.exp(row_peak - new_peak)
        weights = jnp.exp(scores - new_peak[:, None, :])
        new_total = row_total * factor + jnp.sum(weights, axis=1)
        update = jnp.einsum(
            "khd,hkb->hdb",
            value_heads,
            weights.astype(jnp.bfloat16),
            preferred_element_type=jnp.float32,
        )
        return (new_peak, new_total, weighted * factor[:, None, :] + update)

    start_state = (
        jnp.full((HEADS, band_len), -1e30, jnp.float32),
        jnp.zeros((HEADS, band_len), jnp.float32),
        jnp.zeros((HEADS, HEAD_DIM, band_len), jnp.float32),
    )
    softmax_state = attend(start_state, slot_pairs)
    band_count = lax.axis_size("patch")

    def one_side(step_index, packed):
        state_now, ahead = packed
        ahead = banded_advance(ahead)
        return (attend(state_now, ahead), ahead)

    softmax_state, _ = lax.fori_loop(0, band_count - 1, one_side, (softmax_state, slot_pairs))
    _, row_total, weighted = banded_merged(softmax_state, ("chan", "sub"), banded_combine_parts)
    attended = (
        (weighted / row_total[:, None, :]).reshape(HEADS * HEAD_DIM, band_len).astype(jnp.bfloat16)
    )
    mixed = (
        projected.astype(jnp.float32) + jnp.dot(out_w, attended, preferred_element_type=jnp.float32)
    ).astype(jnp.bfloat16)
    columns = proj_out_w
    final_sum = resnet.astype(jnp.float32) + jnp.dot(
        columns,
        lax.all_gather(mixed, ("chan", "sub"), axis=0, tiled=True),
        preferred_element_type=jnp.float32,
    )
    return final_sum.astype(jnp.bfloat16)


def solution(mesh):
    in_specs = (
        P(("chan", "sub"), ("groups", "patch")),
        P("groups"),
        P(),
        P(("chan", "sub"), None),
        P(None, ("chan", "sub"), None),
        P(None, ("chan", "sub"), None),
        P(("chan", "sub"), None),
        P(("chan", "sub"), None),
        P(None, ("chan", "sub"), None),
        P(("chan", "sub"), None),
        P(("chan", "sub"), None),
    )
    out_specs = P(("chan", "sub"), ("groups", "patch"))

    few = mesh.shape["patch"] in (1, 2, 4) and mesh.shape["chan"] == 2 and mesh.shape["sub"] == 2

    def local(latent, *rest):
        if not few or latent.shape[1] != WIDTH:
            return banded(latent, *rest)
        return whole_rows(latent, *rest)

    return jax.shard_map(local, mesh=mesh, in_specs=in_specs, out_specs=out_specs, check_vma=False)
```

```python
import functools
import math

import jax
import jax.numpy as jnp
from jax import lax
from jax.experimental import pallas as pl
from jax.experimental.pallas import tpu as pltpu
from jax.sharding import PartitionSpec as P


C = 640
HEADS = 10
HEAD_DIM = 64
NGROUPS = 32
GROUP = C // NGROUPS
FREQ = 320
WIDTH = 256
BF16 = jnp.bfloat16
F32 = jnp.float32

OWN = C // 4
CHUNK = OWN // 2
FLIPS = (0, 2, 1, 3)


def own_place():
    return lax.axis_index("chan") * 2 + lax.axis_index("sub")


def call(kernel, outs, *args, scratch=(), flops=0, limit=24):
    specs = [pl.BlockSpec(memory_space=pltpu.VMEM)] * len(args)
    moved = sum(math.prod(a.shape) * a.dtype.itemsize for a in args)
    return pl.pallas_call(
        kernel,
        out_shape=[jax.ShapeDtypeStruct(s, t) for s, t in outs],
        in_specs=specs,
        out_specs=[pl.BlockSpec(memory_space=pltpu.VMEM)] * len(outs),
        scratch_shapes=[pltpu.VMEM(s, t) for s, t in scratch],
        compiler_params=pltpu.CompilerParams(vmem_limit_bytes=limit << 20),
        cost_estimate=pl.CostEstimate(flops=flops, transcendentals=0, bytes_accessed=moved),
    )(*args)


def group_sums(sums):
    wide = jnp.broadcast_to(sums, (sums.shape[0], 128))
    row = lax.broadcasted_iota(jnp.int32, wide.shape, 0)
    result = jnp.zeros_like(wide)
    for start in range(0, wide.shape[0], GROUP):
        inside = (row >= start) & (row < start + GROUP)
        total = jnp.sum(jnp.where(inside, wide, 0.0), axis=0, keepdims=True)
        result = jnp.where(inside, total, result)
    return result[:, :1]


def normal_form(rows, epsilon):
    cell_count = GROUP * len(rows) * rows[0].shape[1]
    centre = group_sums(sum(jnp.sum(row, axis=1, keepdims=True) for row in rows)) / cell_count
    shifted = [row - centre for row in rows]
    spread = group_sums(sum(jnp.sum(row * row, axis=1, keepdims=True) for row in shifted))
    scale = lax.rsqrt(spread / cell_count + epsilon)
    return [row * scale for row in shifted]


def silu(values):
    return values * jax.nn.sigmoid(values)


def first_norm(*refs):
    rows_ref, *chunk_refs = refs[-3:]
    pieces = refs[:-3]
    count = len(pieces) // 2
    position = lax.axis_index("patch")
    places = [position ^ by for by in range(count)]
    for piece, place in zip(pieces, places):
        rows_ref[place] = piece[...]
    for part, out in enumerate(chunk_refs):
        for side in range(2):
            values = [
                piece[part * CHUNK : (part + 1) * CHUNK, :].astype(F32)
                for piece in pieces[side * count : (side + 1) * count]
            ]
            for value, place in zip(normal_form(values, 1e-05), places):
                out[side, place] = silu(value).astype(BF16)


def arrange(weight, half_ref, *rest_refs):
    for tap in range(9):
        i, j = divmod(tap, 3)
        for part, rest_ref in enumerate(rest_refs):
            source = weight[tap, part * CHUNK : (part + 1) * CHUNK, :]
            for block in range(4):
                at = block * OWN
                to = (i * 4 + block) * CHUNK
                row = (part * 3 + j) * CHUNK
                half_ref[row : row + CHUNK, to : to + CHUNK] = source[:, at : at + CHUNK]
                row, at = j * CHUNK, at + CHUNK
                rest_ref[row : row + CHUNK, to : to + CHUNK] = source[:, at : at + CHUNK]


def place_blocks(blocks, padded):
    if len(blocks) == 2:
        blocks = [block.at[side] for block in blocks for side in range(2)]
    rows = blocks[0].shape[0]
    edge = jnp.zeros(padded.shape[1:], padded.dtype)
    padded[0] = edge
    padded[rows + 1] = edge
    for flip, block in zip(FLIPS, blocks):
        at = pl.multiple_of((own_place() ^ flip) * CHUNK, 16)
        padded[1 : rows + 1, pl.ds(at, CHUNK), :] = block[...]


def taps(weight, padded, row):
    window = padded[row : row + 3].reshape(3 * 4 * CHUNK, WIDTH)
    every = jnp.dot(weight[...], window, preferred_element_type=F32)
    lane = lax.broadcasted_iota(jnp.int32, (CHUNK, WIDTH), 1)
    results = []
    for start in range(0, every.shape[0], 3 * CHUNK):
        left, here, right = (
            every[start + j * CHUNK : start + (j + 1) * CHUNK] for j in range(3)
        )
        left = jnp.where(lane == 0, 0.0, pltpu.roll(left, 1, 1))
        right = jnp.where(lane == WIDTH - 1, 0.0, pltpu.roll(right, WIDTH - 1, 1))
        results.append(here + left + right)
    return results


def half_conv(*refs):
    *blocks, weight, one_ref, two_ref, padded = refs
    place_blocks(blocks, padded)
    for row in range(one_ref.shape[0]):
        one_ref[row], two_ref[row] = taps(weight, padded, row)


def first_conv(part):
    def kernel(*refs):
        *blocks, weight, half, bias, act_ref, padded = refs
        place_blocks(blocks, padded)
        added = bias[part * CHUNK : (part + 1) * CHUNK, :]
        rows = []
        for row in range(act_ref.shape[0]):
            (rest,) = taps(weight, padded, row)
            rows.append((half[row] + rest + added).astype(BF16).astype(F32))
        for row, value in enumerate(normal_form(rows, 1e-05)):
            act_ref[row] = silu(value).astype(BF16)

    return kernel


def second_conv(part):
    def kernel(*refs):
        *blocks, weight, half, latent, act_ref, resnet_ref, padded, sums = refs
        place_blocks(blocks, padded)
        rows = []
        for row in range(act_ref.shape[0]):
            (rest,) = taps(weight, padded, row)
            value = latent[row, part * CHUNK : (part + 1) * CHUNK, :].astype(F32) + (half[row] + rest)
            value = value.astype(BF16)
            sums[row] = value
            rows.append(value.astype(F32))
        resnet_ref[...] = sums[lax.axis_index("patch")]
        for row, value in enumerate(normal_form(rows, 1e-06)):
            act_ref[row] = value.astype(BF16)

    return kernel


def stack_rows(own, chan, sub, both, full):
    for flip, block in zip(FLIPS, (own, chan, sub, both)):
        full[pl.ds(pl.multiple_of((own_place() ^ flip) * OWN, 16), OWN), :] = block[...]


def stack_heads(q_own, kv_own, q_sub, kv_sub, q_ref, kv_ref):
    here = lax.axis_index("sub") * OWN
    for at, q_part, kv_part in ((here, q_own, kv_own), (OWN - here, q_sub, kv_sub)):
        at = pl.multiple_of(at, 16)
        q_ref[pl.ds(at, OWN), :] = q_part[...]
        kv_ref[pl.ds(at, OWN), :] = kv_part[0]
        kv_ref[pl.ds(at + 2 * OWN, OWN), :] = kv_part[1]


def over_rows(values, combine):
    return combine(
        combine(values.reshape(-1, 8, values.shape[1]), axis=0), axis=0, keepdims=True
    )


def attend(*refs):
    blocks, refs = refs[:8], refs[8:]
    proj_w, q_w, kv_w, out_ref, proj_ref, normed, projected, layered, heads, queries, scores, probs = refs
    rows = normed.shape[0]
    for half in range(2):
        for flip, block in zip(FLIPS, blocks[half * 4 : half * 4 + 4]):
            at = pl.multiple_of((own_place() ^ flip) * OWN + half * CHUNK, 16)
            normed[:, pl.ds(at, CHUNK), :] = block[...]
    halves = [slice(0, C // 2), slice(C // 2, C)]
    for row in range(rows):
        for half in halves:
            projected[row, half, :] = jnp.dot(
                proj_w[half, :], normed[row], preferred_element_type=F32
            ).astype(BF16)
    for row in range(rows):
        value = projected[row].astype(F32)
        shifted = value - over_rows(value, jnp.sum) / C
        spread = over_rows(shifted * shifted, jnp.sum) / C
        layered[row] = (shifted * lax.rsqrt(spread + 1e-05)).astype(BF16)
        at = slice(row * WIDTH, (row + 1) * WIDTH)
        for half in halves:
            heads[half, at] = jnp.dot(
                kv_w[half, :], layered[row], preferred_element_type=F32
            ).astype(BF16)
    proj_ref[...] = projected[lax.axis_index("patch")]
    share = out_ref.shape[1]
    mine = layered[lax.axis_index("patch"), :, pl.ds(pl.multiple_of(lax.axis_index("sub") * share, 128), share)]
    query = (jnp.dot(q_w[...], mine, preferred_element_type=F32) * 0.125).astype(BF16)
    queries[...] = query
    channels = query.shape[0]
    count = channels // HEAD_DIM

    def score(head):
        at = slice(head * HEAD_DIM, (head + 1) * HEAD_DIM)
        scores[head % 2] = lax.dot_general(
            heads[at, :], queries[at, :], (((0,), (0,)), ((), ())), preferred_element_type=F32
        )

    score(0)
    for head in range(count):
        if head + 1 < count:
            score(head + 1)
        parts = [slice(at, at + WIDTH) for at in range(0, rows * WIDTH, WIDTH)]
        peak = functools.reduce(
            jnp.maximum, [over_rows(scores[head % 2, part, :], jnp.max) for part in parts]
        )
        total = 0.0
        for part in parts:
            weights = jnp.exp(scores[head % 2, part, :] - peak)
            total = total + over_rows(weights, jnp.sum)
            probs[head % 2, part, :] = weights.astype(BF16)
        at = channels + head * HEAD_DIM
        weighted = jnp.dot(
            heads[at : at + HEAD_DIM, :], probs[head % 2], preferred_element_type=F32
        )
        out_ref[head * HEAD_DIM : (head + 1) * HEAD_DIM, :] = (weighted / total).astype(BF16)


def fold(proj, res_one, res_two, out_w, last_w, folded_ref, base_ref):
    folded_ref[...] = jnp.dot(
        last_w[...], out_w[...], preferred_element_type=F32
    ).astype(BF16)
    base = jnp.dot(last_w[...], proj[...], preferred_element_type=F32)
    for part, res in enumerate((res_one, res_two)):
        at = slice(part * CHUNK, (part + 1) * CHUNK)
        base_ref[at, :] = res[...].astype(F32) + base[at]


def finish(own, chan, sub, both, folded, base, out_ref, attended):
    channels, share = own.shape
    for flip, block in zip(FLIPS, (own, chan, sub, both)):
        place = own_place() ^ flip
        at = pl.multiple_of((place >> 1) * channels, 16)
        lanes = pl.multiple_of((place & 1) * share, 128)
        attended[pl.ds(at, channels), pl.ds(lanes, share)] = block[...]
    last = jnp.dot(folded[...], attended[...], preferred_element_type=F32)
    out_ref[...] = (base[...] + last).astype(BF16)


def swapped(array, axis, by=1):
    return lax.ppermute(array, axis, [(i, i ^ by) for i in range(lax.axis_size(axis))])


def embedding_of(timestep):
    half_width = FREQ // 2
    frequency = jnp.exp(-math.log(10000.0) * jnp.arange(half_width, dtype=F32) / half_width)
    angles = timestep[0].astype(F32) * frequency
    return jnp.concatenate([jnp.cos(angles), jnp.sin(angles)]).astype(BF16)


def time_bias(embedded, time_w1, time_proj, bias_ref):
    contract_last = (((1,), (1,)), ((), ()))
    wide = jnp.broadcast_to(embedded[...], (16, FREQ))
    hidden = silu(jnp.dot(wide, time_w1[...], preferred_element_type=F32))
    act = silu(hidden).astype(BF16)
    bias_ref[...] = lax.dot_general(
        time_proj[...], act, contract_last, preferred_element_type=F32
    )[:, :1]


def whole_rows(
    latent, timestep, time_w1, time_proj, conv1_w, conv2_w, proj_in_w, q_w, kv_w, out_w, proj_out_w
):
    rows = lax.axis_size("patch")
    chunk = (rows, CHUNK, WIDTH)
    padded = ((rows + 2, 4 * CHUNK, WIDTH), BF16)
    tap_flops = 2 * 3 * CHUNK * 12 * CHUNK * rows * WIDTH
    barrier = lax.optimization_barrier

    def arranged(weight):
        outs = [((width * CHUNK, 12 * CHUNK), BF16) for width in (6, 3, 3)]
        return call(arrange, outs, weight, flops=10**9)

    def stacked(blocks):
        return call(stack_rows, [((C, C), BF16)], *blocks, flops=10**8)[0]

    def exchanged(own, *beside):
        chan = swapped(own, "chan")
        own, chan, beside = barrier((own, chan, beside))
        sub = swapped(own, "sub")
        return (own, chan, sub, swapped(chan, "sub")), beside

    pieces = [latent] + [swapped(latent, "patch", by) for by in range(1, rows)]
    others = [swapped(piece, "chan") for piece in pieces]
    proj_in_chan = swapped(proj_in_w, "chan")
    _, timestep, *heads_w = barrier((pieces[-1], timestep, q_w, kv_w))
    embedded = embedding_of(timestep)[None]
    heads_w = (*heads_w, *(swapped(weight, "sub") for weight in heads_w))
    others, conv1_w, embedded = barrier((others, arranged(conv1_w), embedded))
    pair = (2,) + chunk
    latent_rows, one, two = call(
        first_norm, [((rows, OWN, WIDTH), BF16), (pair, BF16), (pair, BF16)], *pieces, *others,
    )
    one, two = (one, swapped(one, "sub")), (two, swapped(two, "sub"))
    (bias,) = call(time_bias, [((OWN, 1), F32)], embedded, time_w1.T, time_proj, flops=10**8)

    def halves(blocks, weight):
        return call(
            half_conv, [(chunk, F32)] * 2, *blocks, weight, scratch=[padded],
            flops=2 * tap_flops,
        )

    half = halves(one, conv1_w[0])
    one, two = (
        call(
            first_conv(part), [(chunk, BF16)], *two, conv1_w[1 + part], half[part], bias,
            scratch=[padded], flops=tap_flops,
        )[0]
        for part in range(2)
    )
    _, heads_w, conv2_w = barrier((one, heads_w, conv2_w))
    heads_w = call(
        stack_heads, [((2 * OWN, C), BF16), ((4 * OWN, C), BF16)], *heads_w,
        flops=10**8,
    )
    proj_in_sub = swapped(proj_in_w, "sub")
    one, (heads_w, conv2_w, proj_in_sub) = exchanged(one, heads_w, arranged(conv2_w), proj_in_sub)
    two, _ = exchanged(two)
    half = halves(one, conv2_w[0])
    (one, res_one), (two, res_two) = (
        call(
            second_conv(part), [(chunk, BF16), ((CHUNK, WIDTH), BF16)],
            *two, conv2_w[1 + part], half[part], latent_rows,
            scratch=[padded, (chunk, BF16)], flops=tap_flops,
        )
        for part in range(2)
    )
    _, proj_in_chan, out_w = barrier((one, proj_in_chan, out_w))
    proj_in = (proj_in_w, proj_in_chan, proj_in_sub, swapped(proj_in_chan, "sub"))
    one, (proj_in, out_sub) = exchanged(one, stacked(proj_in), swapped(out_w, "sub"))
    two, _ = exchanged(two)
    out_chan = swapped(out_w, "chan")
    share = WIDTH // 2
    attended, projected = call(
        attend, [((2 * OWN, share), BF16), ((C, WIDTH), BF16)],
        *one, *two, proj_in, *heads_w,
        scratch=[((rows, C, WIDTH), BF16)] * 3 + [
            ((4 * OWN, rows * WIDTH), BF16), ((2 * OWN, share), BF16),
            ((2, rows * WIDTH, share), F32), ((2, rows * WIDTH, share), BF16),
        ],
        flops=4 * 10**9, limit=32,
    )
    _, out_chan = barrier((attended, out_chan))
    out_all = stacked((out_w, out_chan, out_sub, swapped(out_chan, "sub")))
    folded = call(
        fold, [((OWN, C), BF16), ((OWN, WIDTH), F32)], projected, res_one, res_two,
        out_all, proj_out_w, flops=10**8,
    )
    attended, folded = exchanged(attended, *folded)
    return call(
        finish, [((OWN, WIDTH), BF16)], *attended, *folded,
        scratch=[((C, WIDTH), BF16)],
    )[0]


def banded_with_halo(cells, sides, width):
    for axis, dim in sides:
        count = lax.axis_size(axis)
        ends = count - 1
        head = lax.slice_in_dim(cells, 0, width, axis=dim)
        tail = lax.slice_in_dim(cells, cells.shape[dim] - width, cells.shape[dim], axis=dim)
        cells = jnp.concatenate(
            [
                lax.ppermute(tail, axis, [(i, (i + 1) % count) for i in range(ends)]),
                cells,
                lax.ppermute(head, axis, [((i + 1) % count, i) for i in range(ends)]),
            ],
            axis=dim,
        )
    return cells


def banded_from_behind(array, axis, by):
    count = lax.axis_size(axis)
    return lax.ppermute(array, axis, [(i, (i + by) % count) for i in range(count)])


def banded_merged(array, axis, combine):
    everything = jax.tree.map(lambda part: lax.all_gather(part, axis), array)
    first = jax.tree.map(lambda part: part[0], everything)

    def turn(k, so_far):
        return combine(so_far, jax.tree.map(lambda part: part[k], everything))

    return lax.fori_loop(1, lax.axis_size(axis), turn, first)


def banded_group_norm(values, epsilon):
    channels, band_len = values.shape
    group_size = C // NGROUPS
    grouped = values.reshape(channels // group_size, group_size, band_len)
    cell_count = group_size * band_len * lax.axis_size("patch")
    centre = lax.psum(jnp.sum(grouped, axis=(1, 2)), "patch") / cell_count
    shifted = grouped - centre[:, None, None]
    spread = lax.psum(jnp.sum(shifted * shifted, axis=(1, 2)), "patch") / cell_count
    normal_form = (grouped - centre[:, None, None]) * lax.rsqrt(spread + epsilon)[:, None, None]
    return normal_form.reshape(channels, band_len)


def banded_convolve(active, weight):
    _, band_len = active.shape
    height = band_len // WIDTH
    whole_rows = lax.all_gather(active, ("chan", "sub"), axis=0, tiled=True)
    image_grid = whole_rows.reshape(whole_rows.shape[0], height, WIDTH)
    padded = banded_with_halo(image_grid, (("patch", 1),), 1)
    channels = padded.shape[0]
    padded = jnp.pad(padded, ((0, 0), (0, 0), (1, 1)))
    running = jnp.zeros((weight.shape[1], band_len), jnp.float32)
    for offset in range(9):
        row_step, col_step = divmod(offset, 3)
        window = padded[:, row_step : row_step + height, col_step : col_step + WIDTH].reshape(
            channels, band_len
        )
        running = running + jnp.dot(weight[offset], window, preferred_element_type=jnp.float32)
    return running


def banded_combine_parts(earlier_part, later_part):
    peak_one, total_one, sums_one = earlier_part
    peak_two, total_two, sums_two = later_part
    new_peak = jnp.maximum(peak_one, peak_two)
    factor_one = jnp.exp(peak_one - new_peak)
    factor_two = jnp.exp(peak_two - new_peak)
    new_total = total_one * factor_one + total_two * factor_two
    new_sums = sums_one * factor_one[:, None, :] + sums_two * factor_two[:, None, :]
    return (new_peak, new_total, new_sums)


def banded_advance(kv_piece):
    return banded_from_behind(kv_piece, "patch", 1)


def banded(
    latent, timestep, time_w1, time_proj, conv1_w, conv2_w, proj_in_w, q_w, kv_w, out_w, proj_out_w
):
    latent_f32 = latent.astype(jnp.float32)
    band_len = latent.shape[1]
    half_width = FREQ // 2
    frequency = jnp.exp(-math.log(10000.0) * jnp.arange(half_width, dtype=jnp.float32) / half_width)
    angles = timestep[0].astype(jnp.float32) * frequency
    embedded = jnp.concatenate([jnp.cos(angles), jnp.sin(angles)]).astype(jnp.bfloat16)
    time_hidden = jax.nn.silu(jnp.dot(time_w1, embedded, preferred_element_type=jnp.float32))
    time_bias = jnp.dot(
        time_proj, jax.nn.silu(time_hidden).astype(jnp.bfloat16), preferred_element_type=jnp.float32
    )
    act_one = jax.nn.silu(banded_group_norm(latent_f32, 1e-05)).astype(jnp.bfloat16)
    conv_one = (banded_convolve(act_one, conv1_w) + time_bias[:, None]).astype(jnp.bfloat16)
    act_two = jax.nn.silu(banded_group_norm(conv_one.astype(jnp.float32), 1e-05)).astype(jnp.bfloat16)
    resnet = (latent_f32 + banded_convolve(act_two, conv2_w)).astype(jnp.bfloat16)
    normed = banded_group_norm(resnet.astype(jnp.float32), 1e-06).astype(jnp.bfloat16)
    columns = proj_in_w
    projected = jnp.dot(
        columns,
        lax.all_gather(normed, ("chan", "sub"), axis=0, tiled=True),
        preferred_element_type=jnp.float32,
    ).astype(jnp.bfloat16)
    whole_proj = lax.all_gather(projected, ("chan", "sub"), axis=0, tiled=True).astype(jnp.float32)
    centre = jnp.mean(whole_proj, axis=0, keepdims=True)
    spread = jnp.mean((whole_proj - centre) * (whole_proj - centre), axis=0, keepdims=True)
    layer_normed = ((whole_proj - centre) / jnp.sqrt(spread + 1e-05)).astype(jnp.bfloat16)
    query_own = (jnp.dot(q_w, layer_normed, preferred_element_type=jnp.float32) * 0.125).astype(
        jnp.bfloat16
    )
    queries = lax.all_gather(query_own, ("chan", "sub"), axis=0, tiled=True).reshape(
        HEADS, HEAD_DIM, band_len
    )
    key_value = jnp.einsum(
        "joc,cb->jbo", kv_w, layer_normed, preferred_element_type=jnp.float32
    ).astype(jnp.bfloat16)
    slot_pairs = lax.all_to_all(key_value, ("chan", "sub"), split_axis=1, concat_axis=2, tiled=True)

    def attend(softmax_state, kv_piece):
        row_peak, row_total, weighted = softmax_state
        slot_len = kv_piece.shape[1]
        key_heads = kv_piece[0].reshape(slot_len, HEADS, HEAD_DIM)
        value_heads = kv_piece[1].reshape(slot_len, HEADS, HEAD_DIM)
        scores = jnp.einsum("khd,hdb->hkb", key_heads, queries, preferred_element_type=jnp.float32)
        new_peak = jnp.maximum(row_peak, jnp.max(scores, axis=1))
        factor = jnp.exp(row_peak - new_peak)
        weights = jnp.exp(scores - new_peak[:, None, :])
        new_total = row_total * factor + jnp.sum(weights, axis=1)
        update = jnp.einsum(
            "khd,hkb->hdb",
            value_heads,
            weights.astype(jnp.bfloat16),
            preferred_element_type=jnp.float32,
        )
        return (new_peak, new_total, weighted * factor[:, None, :] + update)

    start_state = (
        jnp.full((HEADS, band_len), -1e30, jnp.float32),
        jnp.zeros((HEADS, band_len), jnp.float32),
        jnp.zeros((HEADS, HEAD_DIM, band_len), jnp.float32),
    )
    softmax_state = attend(start_state, slot_pairs)
    band_count = lax.axis_size("patch")

    def one_side(step_index, packed):
        state_now, ahead = packed
        ahead = banded_advance(ahead)
        return (attend(state_now, ahead), ahead)

    softmax_state, _ = lax.fori_loop(0, band_count - 1, one_side, (softmax_state, slot_pairs))
    _, row_total, weighted = banded_merged(softmax_state, ("chan", "sub"), banded_combine_parts)
    attended = (
        (weighted / row_total[:, None, :]).reshape(HEADS * HEAD_DIM, band_len).astype(jnp.bfloat16)
    )
    mixed = (
        projected.astype(jnp.float32) + jnp.dot(out_w, attended, preferred_element_type=jnp.float32)
    ).astype(jnp.bfloat16)
    columns = proj_out_w
    final_sum = resnet.astype(jnp.float32) + jnp.dot(
        columns,
        lax.all_gather(mixed, ("chan", "sub"), axis=0, tiled=True),
        preferred_element_type=jnp.float32,
    )
    return final_sum.astype(jnp.bfloat16)


def solution(mesh):
    in_specs = (
        P(("chan", "sub"), ("groups", "patch")),
        P("groups"),
        P(),
        P(("chan", "sub"), None),
        P(None, ("chan", "sub"), None),
        P(None, ("chan", "sub"), None),
        P(("chan", "sub"), None),
        P(("chan", "sub"), None),
        P(None, ("chan", "sub"), None),
        P(("chan", "sub"), None),
        P(("chan", "sub"), None),
    )
    out_specs = P(("chan", "sub"), ("groups", "patch"))

    few = mesh.shape["patch"] in (1, 2, 4) and mesh.shape["chan"] == 2 and mesh.shape["sub"] == 2

    def local(latent, *rest):
        if not few or latent.shape[1] != WIDTH:
            return banded(latent, *rest)
        return whole_rows(latent, *rest)

    return jax.shard_map(local, mesh=mesh, in_specs=in_specs, out_specs=out_specs, check_vma=False)
```

```python
import functools
import math

import jax
import jax.numpy as jnp
from jax import lax
from jax.experimental import pallas as pl
from jax.experimental.pallas import tpu as pltpu
from jax.sharding import PartitionSpec as P


C = 640
HEADS = 10
HEAD_DIM = 64
NGROUPS = 32
GROUP = C // NGROUPS
FREQ = 320
WIDTH = 256
BF16 = jnp.bfloat16
F32 = jnp.float32

OWN = C // 4
CHUNK = OWN // 2
FLIPS = (0, 2, 1, 3)


def own_place():
    return lax.axis_index("chan") * 2 + lax.axis_index("sub")


def call(kernel, outs, *args, scratch=(), flops=0, limit=24):
    specs = [pl.BlockSpec(memory_space=pltpu.VMEM)] * len(args)
    moved = sum(math.prod(a.shape) * a.dtype.itemsize for a in args)
    return pl.pallas_call(
        kernel,
        out_shape=[jax.ShapeDtypeStruct(s, t) for s, t in outs],
        in_specs=specs,
        out_specs=[pl.BlockSpec(memory_space=pltpu.VMEM)] * len(outs),
        scratch_shapes=[pltpu.VMEM(s, t) for s, t in scratch],
        compiler_params=pltpu.CompilerParams(vmem_limit_bytes=limit << 20),
        cost_estimate=pl.CostEstimate(flops=flops, transcendentals=0, bytes_accessed=moved),
    )(*args)


def group_sums(sums):
    wide = jnp.broadcast_to(sums, (sums.shape[0], 128))
    row = lax.broadcasted_iota(jnp.int32, wide.shape, 0)
    result = jnp.zeros_like(wide)
    for start in range(0, wide.shape[0], GROUP):
        inside = (row >= start) & (row < start + GROUP)
        total = jnp.sum(jnp.where(inside, wide, 0.0), axis=0, keepdims=True)
        result = jnp.where(inside, total, result)
    return result[:, :1]


def normal_form(rows, epsilon):
    cell_count = GROUP * len(rows) * rows[0].shape[1]
    centre = group_sums(sum(jnp.sum(row, axis=1, keepdims=True) for row in rows)) / cell_count
    shifted = [row - centre for row in rows]
    spread = group_sums(sum(jnp.sum(row * row, axis=1, keepdims=True) for row in shifted))
    scale = lax.rsqrt(spread / cell_count + epsilon)
    return [row * scale for row in shifted]


def silu(values):
    return values * jax.nn.sigmoid(values)


def first_norm(part):
    def kernel(*refs):
        *pieces, out = refs
        count = len(pieces) // 2
        position = lax.axis_index("patch")
        for side in range(2):
            values = [
                piece[part * CHUNK : (part + 1) * CHUNK, :].astype(F32)
                for piece in pieces[side * count : (side + 1) * count]
            ]
            for by, value in enumerate(normal_form(values, 1e-05)):
                out[side, position ^ by] = silu(value).astype(BF16)

    return kernel


def order_rows(*refs):
    *pieces, rows_ref = refs
    for by, piece in enumerate(pieces):
        rows_ref[lax.axis_index("patch") ^ by] = piece[...]


def arrange(weight, half_ref, *rest_refs):
    for tap in range(9):
        i, j = divmod(tap, 3)
        for part, rest_ref in enumerate(rest_refs):
            source = weight[tap, part * CHUNK : (part + 1) * CHUNK, :]
            for block in range(4):
                at = block * OWN
                to = (i * 4 + block) * CHUNK
                row = (part * 3 + j) * CHUNK
                half_ref[row : row + CHUNK, to : to + CHUNK] = source[:, at : at + CHUNK]
                row, at = j * CHUNK, at + CHUNK
                rest_ref[row : row + CHUNK, to : to + CHUNK] = source[:, at : at + CHUNK]


def place_blocks(blocks, padded):
    if len(blocks) == 2:
        blocks = [block.at[side] for block in blocks for side in range(2)]
    rows = blocks[0].shape[0]
    edge = jnp.zeros(padded.shape[1:], padded.dtype)
    padded[0] = edge
    padded[rows + 1] = edge
    for flip, block in zip(FLIPS, blocks):
        at = pl.multiple_of((own_place() ^ flip) * CHUNK, 16)
        padded[1 : rows + 1, pl.ds(at, CHUNK), :] = block[...]


def taps(weight, padded, row):
    window = padded[row : row + 3].reshape(3 * 4 * CHUNK, WIDTH)
    every = jnp.dot(weight[...], window, preferred_element_type=F32)
    lane = lax.broadcasted_iota(jnp.int32, (CHUNK, WIDTH), 1)
    results = []
    for start in range(0, every.shape[0], 3 * CHUNK):
        left, here, right = (
            every[start + j * CHUNK : start + (j + 1) * CHUNK] for j in range(3)
        )
        left = jnp.where(lane == 0, 0.0, pltpu.roll(left, 1, 1))
        right = jnp.where(lane == WIDTH - 1, 0.0, pltpu.roll(right, WIDTH - 1, 1))
        results.append(here + left + right)
    return results


def half_conv(*refs):
    *blocks, weight, one_ref, two_ref, padded = refs
    place_blocks(blocks, padded)
    for row in range(one_ref.shape[0]):
        one_ref[row], two_ref[row] = taps(weight, padded, row)


def first_conv(part):
    def kernel(*refs):
        *blocks, weight, half, bias, act_ref, padded = refs
        place_blocks(blocks, padded)
        added = bias[part * CHUNK : (part + 1) * CHUNK, :]
        rows = []
        for row in range(act_ref.shape[0]):
            (rest,) = taps(weight, padded, row)
            rows.append((half[row] + rest + added).astype(BF16).astype(F32))
        for row, value in enumerate(normal_form(rows, 1e-05)):
            act_ref[row] = silu(value).astype(BF16)

    return kernel


def second_conv(part):
    def kernel(*refs):
        *blocks, weight, half, latent, act_ref, resnet_ref, padded, sums = refs
        place_blocks(blocks, padded)
        rows = []
        for row in range(act_ref.shape[0]):
            (rest,) = taps(weight, padded, row)
            value = latent[row, part * CHUNK : (part + 1) * CHUNK, :].astype(F32) + (half[row] + rest)
            value = value.astype(BF16)
            sums[row] = value
            rows.append(value.astype(F32))
        resnet_ref[...] = sums[lax.axis_index("patch")]
        for row, value in enumerate(normal_form(rows, 1e-06)):
            act_ref[row] = value.astype(BF16)

    return kernel


def stack_rows(own, chan, sub, both, full):
    for flip, block in zip(FLIPS, (own, chan, sub, both)):
        full[pl.ds(pl.multiple_of((own_place() ^ flip) * OWN, 16), OWN), :] = block[...]


def stack_heads(q_own, kv_own, q_sub, kv_sub, q_ref, kv_ref):
    here = lax.axis_index("sub") * OWN
    for at, q_part, kv_part in ((here, q_own, kv_own), (OWN - here, q_sub, kv_sub)):
        at = pl.multiple_of(at, 16)
        q_ref[pl.ds(at, OWN), :] = q_part[...]
        kv_ref[pl.ds(at, OWN), :] = kv_part[0]
        kv_ref[pl.ds(at + 2 * OWN, OWN), :] = kv_part[1]


def over_rows(values, combine):
    return combine(
        combine(values.reshape(-1, 8, values.shape[1]), axis=0), axis=0, keepdims=True
    )


def attend(*refs):
    blocks, refs = refs[:8], refs[8:]
    proj_w, q_w, kv_w, out_ref, proj_ref, normed, projected, layered, heads, queries, scores, probs = refs
    rows = normed.shape[0]
    for half in range(2):
        for flip, block in zip(FLIPS, blocks[half * 4 : half * 4 + 4]):
            at = pl.multiple_of((own_place() ^ flip) * OWN + half * CHUNK, 16)
            normed[:, pl.ds(at, CHUNK), :] = block[...]
    halves = [slice(0, C // 2), slice(C // 2, C)]
    for row in range(rows):
        for half in halves:
            projected[row, half, :] = jnp.dot(
                proj_w[half, :], normed[row], preferred_element_type=F32
            ).astype(BF16)
    for row in range(rows):
        value = projected[row].astype(F32)
        shifted = value - over_rows(value, jnp.sum) / C
        spread = over_rows(shifted * shifted, jnp.sum) / C
        layered[row] = (shifted * lax.rsqrt(spread + 1e-05)).astype(BF16)
        at = slice(row * WIDTH, (row + 1) * WIDTH)
        for half in halves:
            heads[half, at] = jnp.dot(
                kv_w[half, :], layered[row], preferred_element_type=F32
            ).astype(BF16)
    proj_ref[...] = projected[lax.axis_index("patch")]
    share = out_ref.shape[1]
    mine = layered[lax.axis_index("patch"), :, pl.ds(pl.multiple_of(lax.axis_index("sub") * share, 128), share)]
    query = (jnp.dot(q_w[...], mine, preferred_element_type=F32) * 0.125).astype(BF16)
    queries[...] = query
    channels = query.shape[0]
    count = channels // HEAD_DIM

    def score(head):
        at = slice(head * HEAD_DIM, (head + 1) * HEAD_DIM)
        scores[head % 2] = lax.dot_general(
            heads[at, :], queries[at, :], (((0,), (0,)), ((), ())), preferred_element_type=F32
        )

    score(0)
    for head in range(count):
        if head + 1 < count:
            score(head + 1)
        parts = [slice(at, at + WIDTH) for at in range(0, rows * WIDTH, WIDTH)]
        peak = functools.reduce(
            jnp.maximum, [over_rows(scores[head % 2, part, :], jnp.max) for part in parts]
        )
        total = 0.0
        for part in parts:
            weights = jnp.exp(scores[head % 2, part, :] - peak)
            total = total + over_rows(weights, jnp.sum)
            probs[head % 2, part, :] = weights.astype(BF16)
        at = channels + head * HEAD_DIM
        weighted = jnp.dot(
            heads[at : at + HEAD_DIM, :], probs[head % 2], preferred_element_type=F32
        )
        out_ref[head * HEAD_DIM : (head + 1) * HEAD_DIM, :] = (weighted / total).astype(BF16)


def fold(proj, res_one, res_two, out_w, last_w, folded_ref, base_ref):
    folded_ref[...] = jnp.dot(
        last_w[...], out_w[...], preferred_element_type=F32
    ).astype(BF16)
    base = jnp.dot(last_w[...], proj[...], preferred_element_type=F32)
    for part, res in enumerate((res_one, res_two)):
        at = slice(part * CHUNK, (part + 1) * CHUNK)
        base_ref[at, :] = res[...].astype(F32) + base[at]


def finish(own, chan, sub, both, folded, base, out_ref, attended):
    channels, share = own.shape
    for flip, block in zip(FLIPS, (own, chan, sub, both)):
        place = own_place() ^ flip
        at = pl.multiple_of((place >> 1) * channels, 16)
        lanes = pl.multiple_of((place & 1) * share, 128)
        attended[pl.ds(at, channels), pl.ds(lanes, share)] = block[...]
    last = jnp.dot(folded[...], attended[...], preferred_element_type=F32)
    out_ref[...] = (base[...] + last).astype(BF16)


def swapped(array, axis, by=1):
    return lax.ppermute(array, axis, [(i, i ^ by) for i in range(lax.axis_size(axis))])


def embedding_of(timestep):
    half_width = FREQ // 2
    frequency = jnp.exp(-math.log(10000.0) * jnp.arange(half_width, dtype=F32) / half_width)
    angles = timestep[0].astype(F32) * frequency
    return jnp.concatenate([jnp.cos(angles), jnp.sin(angles)]).astype(BF16)


def time_bias(embedded, time_w1, time_proj, bias_ref):
    contract_last = (((1,), (1,)), ((), ()))
    wide = jnp.broadcast_to(embedded[...], (16, FREQ))
    hidden = silu(jnp.dot(wide, time_w1[...], preferred_element_type=F32))
    act = silu(hidden).astype(BF16)
    bias_ref[...] = lax.dot_general(
        time_proj[...], act, contract_last, preferred_element_type=F32
    )[:, :1]


def whole_rows(
    latent, timestep, time_w1, time_proj, conv1_w, conv2_w, proj_in_w, q_w, kv_w, out_w, proj_out_w
):
    rows = lax.axis_size("patch")
    chunk = (rows, CHUNK, WIDTH)
    padded = ((rows + 2, 4 * CHUNK, WIDTH), BF16)
    tap_flops = 2 * 3 * CHUNK * 12 * CHUNK * rows * WIDTH
    barrier = lax.optimization_barrier

    def arranged(weight):
        outs = [((width * CHUNK, 12 * CHUNK), BF16) for width in (6, 3, 3)]
        return call(arrange, outs, weight, flops=10**9)

    def stacked(blocks):
        return call(stack_rows, [((C, C), BF16)], *blocks, flops=10**8)[0]

    def exchanged(own, *beside):
        chan = swapped(own, "chan")
        own, chan, beside = barrier((own, chan, beside))
        sub = swapped(own, "sub")
        return (own, chan, sub, swapped(chan, "sub")), beside

    pieces = [latent] + [swapped(latent, "patch", by) for by in range(1, rows)]
    others = [swapped(piece, "chan") for piece in pieces]
    proj_in_chan = swapped(proj_in_w, "chan")
    _, timestep, *heads_w = barrier((pieces[-1], timestep, q_w, kv_w))
    embedded = embedding_of(timestep)[None]
    heads_w = (*heads_w, *(swapped(weight, "sub") for weight in heads_w))
    others, conv1_w, embedded = barrier((others, arranged(conv1_w), embedded))
    pair = (2,) + chunk
    one, two = (
        call(first_norm(part), [(pair, BF16)], *pieces, *others)[0]
        for part in range(2)
    )
    one, two = (one, swapped(one, "sub")), (two, swapped(two, "sub"))
    (latent_rows,) = call(order_rows, [((rows, OWN, WIDTH), BF16)], *pieces)
    (bias,) = call(time_bias, [((OWN, 1), F32)], embedded, time_w1.T, time_proj, flops=10**8)

    def halves(blocks, weight):
        return call(
            half_conv, [(chunk, F32)] * 2, *blocks, weight, scratch=[padded],
            flops=2 * tap_flops,
        )

    half = halves(one, conv1_w[0])
    one, two = (
        call(
            first_conv(part), [(chunk, BF16)], *two, conv1_w[1 + part], half[part], bias,
            scratch=[padded], flops=tap_flops,
        )[0]
        for part in range(2)
    )
    _, heads_w, conv2_w = barrier((one, heads_w, conv2_w))
    heads_w = call(
        stack_heads, [((2 * OWN, C), BF16), ((4 * OWN, C), BF16)], *heads_w,
        flops=10**8,
    )
    proj_in_sub = swapped(proj_in_w, "sub")
    one, (heads_w, conv2_w, proj_in_sub) = exchanged(one, heads_w, arranged(conv2_w), proj_in_sub)
    two, _ = exchanged(two)
    half = halves(one, conv2_w[0])
    (one, res_one), (two, res_two) = (
        call(
            second_conv(part), [(chunk, BF16), ((CHUNK, WIDTH), BF16)],
            *two, conv2_w[1 + part], half[part], latent_rows,
            scratch=[padded, (chunk, BF16)], flops=tap_flops,
        )
        for part in range(2)
    )
    _, proj_in_chan, out_w = barrier((one, proj_in_chan, out_w))
    proj_in = (proj_in_w, proj_in_chan, proj_in_sub, swapped(proj_in_chan, "sub"))
    one, (proj_in, out_sub) = exchanged(one, stacked(proj_in), swapped(out_w, "sub"))
    two, _ = exchanged(two)
    out_chan = swapped(out_w, "chan")
    share = WIDTH // 2
    attended, projected = call(
        attend, [((2 * OWN, share), BF16), ((C, WIDTH), BF16)],
        *one, *two, proj_in, *heads_w,
        scratch=[((rows, C, WIDTH), BF16)] * 3 + [
            ((4 * OWN, rows * WIDTH), BF16), ((2 * OWN, share), BF16),
            ((2, rows * WIDTH, share), F32), ((2, rows * WIDTH, share), BF16),
        ],
        flops=4 * 10**9, limit=32,
    )
    _, out_chan = barrier((attended, out_chan))
    out_all = stacked((out_w, out_chan, out_sub, swapped(out_chan, "sub")))
    folded = call(
        fold, [((OWN, C), BF16), ((OWN, WIDTH), F32)], projected, res_one, res_two,
        out_all, proj_out_w, flops=10**8,
    )
    attended, folded = exchanged(attended, *folded)
    return call(
        finish, [((OWN, WIDTH), BF16)], *attended, *folded,
        scratch=[((C, WIDTH), BF16)],
    )[0]


def banded_with_halo(cells, sides, width):
    for axis, dim in sides:
        count = lax.axis_size(axis)
        ends = count - 1
        head = lax.slice_in_dim(cells, 0, width, axis=dim)
        tail = lax.slice_in_dim(cells, cells.shape[dim] - width, cells.shape[dim], axis=dim)
        cells = jnp.concatenate(
            [
                lax.ppermute(tail, axis, [(i, (i + 1) % count) for i in range(ends)]),
                cells,
                lax.ppermute(head, axis, [((i + 1) % count, i) for i in range(ends)]),
            ],
            axis=dim,
        )
    return cells


def banded_from_behind(array, axis, by):
    count = lax.axis_size(axis)
    return lax.ppermute(array, axis, [(i, (i + by) % count) for i in range(count)])


def banded_merged(array, axis, combine):
    everything = jax.tree.map(lambda part: lax.all_gather(part, axis), array)
    first = jax.tree.map(lambda part: part[0], everything)

    def turn(k, so_far):
        return combine(so_far, jax.tree.map(lambda part: part[k], everything))

    return lax.fori_loop(1, lax.axis_size(axis), turn, first)


def banded_group_norm(values, epsilon):
    channels, band_len = values.shape
    group_size = C // NGROUPS
    grouped = values.reshape(channels // group_size, group_size, band_len)
    cell_count = group_size * band_len * lax.axis_size("patch")
    centre = lax.psum(jnp.sum(grouped, axis=(1, 2)), "patch") / cell_count
    shifted = grouped - centre[:, None, None]
    spread = lax.psum(jnp.sum(shifted * shifted, axis=(1, 2)), "patch") / cell_count
    normal_form = (grouped - centre[:, None, None]) * lax.rsqrt(spread + epsilon)[:, None, None]
    return normal_form.reshape(channels, band_len)


def banded_convolve(active, weight):
    _, band_len = active.shape
    height = band_len // WIDTH
    whole_rows = lax.all_gather(active, ("chan", "sub"), axis=0, tiled=True)
    image_grid = whole_rows.reshape(whole_rows.shape[0], height, WIDTH)
    padded = banded_with_halo(image_grid, (("patch", 1),), 1)
    channels = padded.shape[0]
    padded = jnp.pad(padded, ((0, 0), (0, 0), (1, 1)))
    running = jnp.zeros((weight.shape[1], band_len), jnp.float32)
    for offset in range(9):
        row_step, col_step = divmod(offset, 3)
        window = padded[:, row_step : row_step + height, col_step : col_step + WIDTH].reshape(
            channels, band_len
        )
        running = running + jnp.dot(weight[offset], window, preferred_element_type=jnp.float32)
    return running


def banded_combine_parts(earlier_part, later_part):
    peak_one, total_one, sums_one = earlier_part
    peak_two, total_two, sums_two = later_part
    new_peak = jnp.maximum(peak_one, peak_two)
    factor_one = jnp.exp(peak_one - new_peak)
    factor_two = jnp.exp(peak_two - new_peak)
    new_total = total_one * factor_one + total_two * factor_two
    new_sums = sums_one * factor_one[:, None, :] + sums_two * factor_two[:, None, :]
    return (new_peak, new_total, new_sums)


def banded_advance(kv_piece):
    return banded_from_behind(kv_piece, "patch", 1)


def banded(
    latent, timestep, time_w1, time_proj, conv1_w, conv2_w, proj_in_w, q_w, kv_w, out_w, proj_out_w
):
    latent_f32 = latent.astype(jnp.float32)
    band_len = latent.shape[1]
    half_width = FREQ // 2
    frequency = jnp.exp(-math.log(10000.0) * jnp.arange(half_width, dtype=jnp.float32) / half_width)
    angles = timestep[0].astype(jnp.float32) * frequency
    embedded = jnp.concatenate([jnp.cos(angles), jnp.sin(angles)]).astype(jnp.bfloat16)
    time_hidden = jax.nn.silu(jnp.dot(time_w1, embedded, preferred_element_type=jnp.float32))
    time_bias = jnp.dot(
        time_proj, jax.nn.silu(time_hidden).astype(jnp.bfloat16), preferred_element_type=jnp.float32
    )
    act_one = jax.nn.silu(banded_group_norm(latent_f32, 1e-05)).astype(jnp.bfloat16)
    conv_one = (banded_convolve(act_one, conv1_w) + time_bias[:, None]).astype(jnp.bfloat16)
    act_two = jax.nn.silu(banded_group_norm(conv_one.astype(jnp.float32), 1e-05)).astype(jnp.bfloat16)
    resnet = (latent_f32 + banded_convolve(act_two, conv2_w)).astype(jnp.bfloat16)
    normed = banded_group_norm(resnet.astype(jnp.float32), 1e-06).astype(jnp.bfloat16)
    columns = proj_in_w
    projected = jnp.dot(
        columns,
        lax.all_gather(normed, ("chan", "sub"), axis=0, tiled=True),
        preferred_element_type=jnp.float32,
    ).astype(jnp.bfloat16)
    whole_proj = lax.all_gather(projected, ("chan", "sub"), axis=0, tiled=True).astype(jnp.float32)
    centre = jnp.mean(whole_proj, axis=0, keepdims=True)
    spread = jnp.mean((whole_proj - centre) * (whole_proj - centre), axis=0, keepdims=True)
    layer_normed = ((whole_proj - centre) / jnp.sqrt(spread + 1e-05)).astype(jnp.bfloat16)
    query_own = (jnp.dot(q_w, layer_normed, preferred_element_type=jnp.float32) * 0.125).astype(
        jnp.bfloat16
    )
    queries = lax.all_gather(query_own, ("chan", "sub"), axis=0, tiled=True).reshape(
        HEADS, HEAD_DIM, band_len
    )
    key_value = jnp.einsum(
        "joc,cb->jbo", kv_w, layer_normed, preferred_element_type=jnp.float32
    ).astype(jnp.bfloat16)
    slot_pairs = lax.all_to_all(key_value, ("chan", "sub"), split_axis=1, concat_axis=2, tiled=True)

    def attend(softmax_state, kv_piece):
        row_peak, row_total, weighted = softmax_state
        slot_len = kv_piece.shape[1]
        key_heads = kv_piece[0].reshape(slot_len, HEADS, HEAD_DIM)
        value_heads = kv_piece[1].reshape(slot_len, HEADS, HEAD_DIM)
        scores = jnp.einsum("khd,hdb->hkb", key_heads, queries, preferred_element_type=jnp.float32)
        new_peak = jnp.maximum(row_peak, jnp.max(scores, axis=1))
        factor = jnp.exp(row_peak - new_peak)
        weights = jnp.exp(scores - new_peak[:, None, :])
        new_total = row_total * factor + jnp.sum(weights, axis=1)
        update = jnp.einsum(
            "khd,hkb->hdb",
            value_heads,
            weights.astype(jnp.bfloat16),
            preferred_element_type=jnp.float32,
        )
        return (new_peak, new_total, weighted * factor[:, None, :] + update)

    start_state = (
        jnp.full((HEADS, band_len), -1e30, jnp.float32),
        jnp.zeros((HEADS, band_len), jnp.float32),
        jnp.zeros((HEADS, HEAD_DIM, band_len), jnp.float32),
    )
    softmax_state = attend(start_state, slot_pairs)
    band_count = lax.axis_size("patch")

    def one_side(step_index, packed):
        state_now, ahead = packed
        ahead = banded_advance(ahead)
        return (attend(state_now, ahead), ahead)

    softmax_state, _ = lax.fori_loop(0, band_count - 1, one_side, (softmax_state, slot_pairs))
    _, row_total, weighted = banded_merged(softmax_state, ("chan", "sub"), banded_combine_parts)
    attended = (
        (weighted / row_total[:, None, :]).reshape(HEADS * HEAD_DIM, band_len).astype(jnp.bfloat16)
    )
    mixed = (
        projected.astype(jnp.float32) + jnp.dot(out_w, attended, preferred_element_type=jnp.float32)
    ).astype(jnp.bfloat16)
    columns = proj_out_w
    final_sum = resnet.astype(jnp.float32) + jnp.dot(
        columns,
        lax.all_gather(mixed, ("chan", "sub"), axis=0, tiled=True),
        preferred_element_type=jnp.float32,
    )
    return final_sum.astype(jnp.bfloat16)


def solution(mesh):
    in_specs = (
        P(("chan", "sub"), ("groups", "patch")),
        P("groups"),
        P(),
        P(("chan", "sub"), None),
        P(None, ("chan", "sub"), None),
        P(None, ("chan", "sub"), None),
        P(("chan", "sub"), None),
        P(("chan", "sub"), None),
        P(None, ("chan", "sub"), None),
        P(("chan", "sub"), None),
        P(("chan", "sub"), None),
    )
    out_specs = P(("chan", "sub"), ("groups", "patch"))

    few = mesh.shape["patch"] in (1, 2, 4) and mesh.shape["chan"] == 2 and mesh.shape["sub"] == 2

    def local(latent, *rest):
        if not few or latent.shape[1] != WIDTH:
            return banded(latent, *rest)
        return whole_rows(latent, *rest)

    return jax.shard_map(local, mesh=mesh, in_specs=in_specs, out_specs=out_specs, check_vma=False)
```
